256 devices in a mesh: cores: 4 (over x), row: 32 (over z, y), tensor: 2 (over core).
Axes of the slice: x: 4, y: 4, z: 8, core: 2. Of those that a mesh axis runs over, the one named last changes fastest.
Arguments:
- cores: float32 [2, 4, 128, 256, 256], P('tensor', 'cores', 'row'), may hold values from -1 to 1, as said below
- incoming: float32 [2, 256, 256], P('tensor'), may hold values from -1 to 2, as said below
Outputs:
- frames: float32 [2, 4, 128, 256, 256], P('tensor', 'cores', 'row')
- tail: float32 [2, 256, 256], P('tensor', 'cores')
- correlation: float32 [2, 256, 256], P('tensor', 'cores')
The draws below stay inside these ranges and needn't reach their ends.
Inputs may be any that keep to these rules, and one draw needn't show every extreme that they name: `cores`: each core's unfolding over (mode index, left rank) has full column rank and is well conditioned. `incoming`: upper triangular, diagonal entries from 1 to 2.
All inputs are finite; a program needn't handle non-finite values.
Results may differ from the reference program's by a relative error of at most 0.0001.
Values sent between devices are 32-bit elements; how exact they have to be, the bound alone decides.
No kernel may reach another device: no remote copies, remote signals or barrier semaphores. Data moves between devices by JAX's collectives and lax.ppermute only.
A program may use at most 64 MiB of HBM per device.

```python
import jax
import jax.numpy as jnp
from jax import lax

RANK = 256
MODE = 128
TRAIN_CORES = 4


def draw_cores(key, part):
    shape = (TRAIN_CORES, MODE, RANK, RANK)
    common = jax.random.normal(jax.random.fold_in(key, 11), (1,) + shape, jnp.float32)
    noise = jax.random.normal(jax.random.fold_in(key, 12), (2,) + shape, jnp.float32)
    mixed_gram = common + 0.3 * noise
    return mixed_gram / jnp.sqrt(1.09 * MODE * RANK)


def draw_incoming(key, part):
    diagonal = jax.random.uniform(jax.random.fold_in(key, 21), (2, RANK), jnp.float32, 1.0, 2.0)
    spread = jax.random.normal(jax.random.fold_in(key, 22), (2, RANK, RANK), jnp.float32) * (0.8 / RANK ** 0.5)
    spread = jnp.clip(spread, -0.9, 0.9)
    strict = jnp.triu(spread, 1)
    return strict + jax.vmap(jnp.diag)(diagonal)


def setup_inputs(seed: int = 0) -> dict:
    arg_keys = jax.random.split(jax.random.key(seed), 3)
    return {
        "cores": draw_cores(jax.random.fold_in(arg_keys[2], 71), 0),
        "incoming": draw_incoming(jax.random.fold_in(arg_keys[2], 71), 0),
    }


HIGH_PRECISION = lax.Precision.HIGHEST

def chain_step(upper, block):
    mixed_gram = jnp.einsum('ab,ibc->iac', upper, block, precision=HIGH_PRECISION)
    gram_matrix = jnp.einsum('bgk,bgj->kj', mixed_gram, mixed_gram, precision=HIGH_PRECISION)
    lower = jnp.linalg.cholesky(gram_matrix)
    identity_matrix = jnp.eye(gram_matrix.shape[0], dtype=gram_matrix.dtype)
    inverse_factor = lax.linalg.triangular_solve(lower, identity_matrix, left_side=True, lower=True)
    basis_frame = jnp.einsum('pwv,kv->pwk', mixed_gram, inverse_factor, precision=HIGH_PRECISION)
    return (basis_frame, lower.T)

def link_step(link, left, right):
    middle = jnp.einsum('bc,icd->ibd', link, right, precision=HIGH_PRECISION)
    return jnp.einsum('iba,ibd->ad', left, middle, precision=HIGH_PRECISION)

def reference(cores, incoming):
    factor = float(MODE * RANK) ** 0.5
    frame_list = []
    tails = []
    correlations = []
    for which in range(2):
        upper = incoming[which]
        blocks = []
        for index in range(TRAIN_CORES):
            basis_frame, upper = chain_step(upper, cores[which, index])
            blocks.append(basis_frame * factor)
        frame_list.append(jnp.stack(blocks))
        tails.append(upper)
        other = 1 - which
        link = jnp.dot(incoming[which].T, incoming[other], precision=HIGH_PRECISION)
        for index in range(TRAIN_CORES):
            link = link_step(link, cores[which, index], cores[other, index])
        correlations.append(link)
    return (jnp.stack(frame_list), jnp.stack(tails), jnp.stack(correlations))
```

```python
import functools

import jax
import jax.numpy as jnp
from jax import lax
from jax.experimental import pallas as pl
from jax.experimental.pallas import tpu as pltpu
from jax.sharding import PartitionSpec as P

MODE = 128
BLOCK = 32
VMEM_LIMIT = 48 * 1024 * 1024
F32 = jnp.float32
BF16 = jnp.bfloat16

VMEM = pl.BlockSpec(memory_space=pltpu.VMEM)
SMEM = pl.BlockSpec(memory_space=pltpu.SMEM)


def call(body, outs, in_specs, scratch=()):
    return pl.pallas_call(
        body,
        out_shape=[jax.ShapeDtypeStruct(s, d) for s, d in outs],
        in_specs=in_specs,
        out_specs=[VMEM] * len(outs),
        scratch_shapes=list(scratch),
        compiler_params=pltpu.CompilerParams(vmem_limit_bytes=VMEM_LIMIT),
    )


def split(x):
    hi = x.astype(BF16)
    return hi, (x - hi.astype(F32)).astype(BF16)


def dot(a, b, dims=((1,), (0,))):
    return lax.dot_general(a, b, (dims, ((), ())), preferred_element_type=F32)


def dot3(a, b, dims=((1,), (0,))):
    (ah, al), (bh, bl) = a, b
    return dot(ah, bh, dims) + (dot(ah, bl, dims) + dot(al, bh, dims))


def full(a, b, dims=((1,), (0,))):
    return lax.dot_general(
        a, b, (dims, ((), ())), precision=lax.Precision.HIGHEST, preferred_element_type=F32
    )


def prepare(which, own, other, up, up_other, ch, cl, th, tl, lh, ll, rh, rl, start, beside):
    first = which[0] == 0
    modes, rank = own.shape[0], own.shape[1]
    half = rank // 2
    for i in range(modes):
        at = pl.ds(i * rank, rank)
        at_half = pl.ds(i * half, half)
        mine = own[i]
        theirs = other[i]
        ch[:, at], cl[:, at] = split(mine)
        th[:, at], tl[:, at] = split(mine.T)
        lh[:, at], ll[:, at] = split(jnp.where(first, mine, theirs).T)
        rh[:, at_half], rl[:, at_half] = split(
            jnp.where(first, theirs[:, :half], mine[:, half:])
        )
    u, v = up[...], up_other[...]
    start[:, :rank] = full(u, u, ((0,), (0,)))
    link = full(jnp.where(first, u, v), jnp.where(first, v, u), ((0,), (0,)))
    start[:, rank:] = jnp.where(first, link[:, :half], link[:, half:])
    beside[...] = jnp.where(first, link[:, half:], link[:, :half])


def chain(which, state, beside, ch, cl, th, tl, lh, ll, rh, rl, out):
    first = which[0] == 0
    rank = ch.shape[0]
    half = rank // 2
    modes = ch.shape[1] // rank
    gram = split(state[:, :rank])
    mine, theirs = state[:, rank:], beside[...]
    link = split(
        jnp.concatenate(
            [jnp.where(first, mine, theirs), jnp.where(first, theirs, mine)], axis=1
        )
    )
    total = jnp.zeros((rank, rank), F32)
    total_link = jnp.zeros((rank, half), F32)
    for i in range(modes):
        at = pl.ds(i * rank, rank)
        at_half = pl.ds(i * half, half)
        middle = split(dot3(gram, (ch[:, at], cl[:, at])))
        total += dot3((th[:, at], tl[:, at]), middle)
        middle = split(dot3(link, (rh[:, at_half], rl[:, at_half])))
        total_link += dot3((lh[:, at], ll[:, at]), middle)
    out[:, :rank] = total
    out[:, rank:] = total_link


def factor(active, gram, u_before, x_before, u_out, x_out, work):
    rank = gram.shape[0]

    @pl.when(active[0] == 0)
    def _():
        u_out[...] = u_before[...]
        x_out[...] = x_before[...]

    @pl.when(active[0] != 0)
    def _():
        rows_all = lax.broadcasted_iota(jnp.int32, (rank, rank), 0)
        cols_all = lax.broadcasted_iota(jnp.int32, (rank, rank), 1)
        work[:, :rank] = gram[:, :rank]
        work[:, rank:] = jnp.where(rows_all == cols_all, 1.0, 0.0).astype(F32)
        rows = lax.broadcasted_iota(jnp.int32, (BLOCK, 128), 0)
        lanes = lax.broadcasted_iota(jnp.int32, (BLOCK, 128), 1)
        for b in range(rank // BLOCK):
            r = b * BLOCK
            tile, offset = r // 128 * 128, r % 128
            m = work[r : r + BLOCK, tile : tile + 128]
            e = jnp.where(rows == lanes, 1.0, 0.0).astype(F32)
            pivots = jnp.ones((BLOCK, 128), F32)
            for j in range(BLOCK):
                column = jnp.broadcast_to(m[:, offset + j : offset + j + 1], (BLOCK, 128))
                pivots = jnp.where(rows == j, column, pivots)
                f = jnp.where(rows > j, column / column[j : j + 1, :], 0.0)
                e = e - f * e[j : j + 1, :]
                m = m - f * m[j : j + 1, :]
            x = e * (1.0 / jnp.sqrt(pivots))
            line = full(x[:, :BLOCK], work[r : r + BLOCK, :])
            upper = jnp.where(
                lax.broadcasted_iota(jnp.int32, (BLOCK, rank), 1)
                >= lax.broadcasted_iota(jnp.int32, (BLOCK, rank), 0) + r,
                line[:, :rank],
                0.0,
            )
            u_out[r : r + BLOCK, :] = upper
            x_out[r : r + BLOCK, :] = line[:, rank:]
            if r + BLOCK < rank:
                update = full(upper, line, ((0,), (0,)))
                work[r + BLOCK :, :] = work[r + BLOCK :, :] - update[r + BLOCK :, :]


def frame(scale, own, upper, inverse, out):
    u = split(upper[...])
    x = split(inverse[...] * scale)
    for i in range(own.shape[0]):
        mixed = split(dot3(u, split(own[i])))
        out[i] = dot3(mixed, x, ((1,), (1,)))


def swapped(x):
    return lax.ppermute(x, "tensor", [(0, 1), (1, 0)])


def moved(x, source, target):
    return lax.ppermute(x, "cores", [(source, target)])


def shards(cores, incoming):
    own, up = cores[0, 0], incoming[0]
    modes, rank, _ = own.shape
    half = rank // 2
    section, which = lax.axis_index("cores"), lax.axis_index("tensor")
    sections, rows = lax.axis_size("cores"), lax.axis_size("row")
    last = sections - 1
    scalar = which.astype(jnp.int32)[None]

    other, up_other = swapped(own), swapped(up)
    wide, narrow = ((rank, modes * rank), BF16), ((rank, modes * half), BF16)
    *parts, state, beside = call(
        prepare,
        [wide] * 6 + [narrow] * 2 + [((rank, rank + half), F32), ((rank, half), F32)],
        [SMEM] + [VMEM] * 4,
    )(scalar, own, other, up, up_other)

    run_chain = call(chain, [((rank, rank + half), F32)], [SMEM] + [VMEM] * 10)
    run_factor = call(
        factor,
        [((rank, rank), F32)] * 2,
        [SMEM] + [VMEM] * 3,
        [pltpu.VMEM((rank, 2 * rank), F32)],
    )
    u_now = x_now = up
    grams = []
    for tick in range(sections):
        (partial,) = run_chain(scalar, state, beside, *parts)
        tiles = partial.reshape(rows, rank // rows, rank + half)
        piece = lax.all_to_all(tiles, "row", 0, 0, tiled=True).sum(axis=0)
        if tick < last:
            piece = jnp.where(section == tick + 1, moved(piece, tick, tick + 1), piece)
        copies = jnp.broadcast_to(piece[None], tiles.shape)
        state = lax.all_to_all(copies, "row", 0, 0, tiled=True).reshape(partial.shape)
        beside = swapped(state[:, rank:])
        grams.append(state)
        if tick == last - 1:
            gram = grams[0]
            for k in range(1, last):
                gram = jnp.where(section == k, grams[k], gram)
            u_now, x_now = run_factor((section < last).astype(jnp.int32)[None], gram, u_now, x_now)
            u_before = lax.ppermute(u_now, "cores", [(k, k + 1) for k in range(last)])
            u_before = jnp.where(section == 0, up, u_before)

    mine = state[:, rank:]
    link = jnp.concatenate(
        [jnp.where(which == 0, mine, beside), jnp.where(which == 0, beside, mine)], axis=1
    )
    link = jnp.where(which == 0, link, link.T)
    u_now, x_now = run_factor((section == last).astype(jnp.int32)[None], state, u_now, x_now)
    (frames,) = call(
        functools.partial(frame, float(MODE * rank) ** 0.5), [(own.shape, F32)], [VMEM] * 3
    )(own, u_before, x_now)
    share = rank // sections

    def spread(x):
        tiles = x.reshape(sections, share, rank)
        result = tiles[last]
        for k in range(last):
            result = jnp.where(section == k, moved(tiles[k], last, k), result)
        return result

    return frames[None, None], spread(u_now)[None], spread(link)[None]


def solution(mesh):
    in_specs = (P("tensor", "cores", "row", None, None), P("tensor", None, None))
    out_specs = (
        P("tensor", "cores", "row", None, None),
        P("tensor", "cores", None),
        P("tensor", "cores", None),
    )
    return jax.shard_map(shards, mesh=mesh, in_specs=in_specs, out_specs=out_specs, check_vma=False)
```

```python
import functools

import jax
import jax.numpy as jnp
from jax import lax
from jax.experimental import pallas as pl
from jax.experimental.pallas import tpu as pltpu
from jax.sharding import PartitionSpec as P

MODE = 128
LANES = 128
BLOCK = 64
GROUP = 8
VMEM_LIMIT = 48 * 1024 * 1024
F32 = jnp.float32
BF16 = jnp.bfloat16

VMEM = pl.BlockSpec(memory_space=pltpu.VMEM)
SMEM = pl.BlockSpec(memory_space=pltpu.SMEM)


def call(body, outs, in_specs, scratch=()):
    return pl.pallas_call(
        body,
        out_shape=[jax.ShapeDtypeStruct(s, d) for s, d in outs],
        in_specs=in_specs,
        out_specs=[VMEM] * len(outs),
        scratch_shapes=list(scratch),
        compiler_params=pltpu.CompilerParams(vmem_limit_bytes=VMEM_LIMIT),
    )


def split(x):
    hi = x.astype(BF16)
    return hi, (x - hi.astype(F32)).astype(BF16)


def dot(a, b, dims=((1,), (0,))):
    return lax.dot_general(a, b, (dims, ((), ())), preferred_element_type=F32)


def dot3(a, b, dims=((1,), (0,))):
    (ah, al), (bh, bl) = a, b
    return dot(ah, bh, dims) + (dot(ah, bl, dims) + dot(al, bh, dims))


def full(a, b, dims=((1,), (0,))):
    return lax.dot_general(
        a, b, (dims, ((), ())), precision=lax.Precision.HIGHEST, preferred_element_type=F32
    )


def pack_gram(out, gram):
    half = gram.shape[0] // 2
    out[0:half, :] = gram[:half, :half]
    out[half : 2 * half, :] = gram[:half, half:]
    out[2 * half : 3 * half, :] = gram[half:, half:]


def gram_blocks(state):
    half = LANES
    return state[0:half, :], state[half : 2 * half, :], state[2 * half : 3 * half, :]


def whole_link(first, mine, theirs):
    return jnp.concatenate(
        [jnp.where(first, mine, theirs), jnp.where(first, theirs, mine)], axis=1
    )


def prepare_own(own, ch, cl, th, tl):
    modes, rank = own.shape[0], own.shape[1]
    for i in range(modes):
        at = pl.ds(i * rank, rank)
        mine = own[i]
        ch[:, at], cl[:, at] = split(mine)
        th[:, at], tl[:, at] = split(mine.T)


def prepare_link(which, own, other, th, tl, up, up_other, lh, ll, rh, rl, start, beside):
    modes, rank = own.shape[0], own.shape[1]
    half = rank // 2
    u, v = up[...], up_other[...]
    pack_gram(start, full(u, u, ((0,), (0,))))

    def sides(left, right, mine, theirs):
        link = full(left, right, ((0,), (0,)))
        start[3 * half :, :] = link[:, mine]
        beside[...] = link[:, theirs]

    low, high = slice(0, half), slice(half, rank)

    @pl.when(which[0] == 0)
    def _():
        lh[...] = th[...]
        ll[...] = tl[...]
        for i in range(modes):
            at = pl.ds(i * half, half)
            rh[:, at], rl[:, at] = split(other[i][:, low])
        sides(u, v, low, high)

    @pl.when(which[0] != 0)
    def _():
        for i in range(modes):
            at = pl.ds(i * half, half)
            rh[:, at], rl[:, at] = split(own[i][:, high])
            at = pl.ds(i * rank, rank)
            lh[:, at], ll[:, at] = split(other[i].T)
        sides(v, u, high, low)


def stacked(x, width):
    return jnp.concatenate(
        [x[:, i : i + width] for i in range(0, x.shape[1], width)], axis=0
    )


def chain_product(middle, right, left, width):
    mh, ml = split(dot3(middle, right))
    return dot3(left, (stacked(mh, width), stacked(ml, width)))


def chain(which, state, beside, ch, cl, th, tl, lh, ll, rh, rl, out):
    rank = ch.shape[0]
    half = rank // 2
    a, b, c = gram_blocks(state)
    gram = jnp.concatenate(
        [jnp.concatenate([a, b], axis=1), jnp.concatenate([b.T, c], axis=1)], axis=0
    )
    pack_gram(out, chain_product(split(gram), (ch[...], cl[...]), (th[...], tl[...]), rank))
    link = whole_link(which[0] == 0, state[3 * half :, :], beside[...])
    out[3 * half :, :] = chain_product(
        split(link), (rh[...], rl[...]), (lh[...], ll[...]), half
    )


def eliminate(m, offset, n):
    rows = lax.broadcasted_iota(jnp.int32, (n, LANES), 0)
    lanes = lax.broadcasted_iota(jnp.int32, (n, LANES), 1)
    e = jnp.where(rows == lanes, 1.0, 0.0).astype(F32)
    done = []
    for g in range(0, n, GROUP):
        left = n - g
        at = lax.broadcasted_iota(jnp.int32, (left, LANES), 0)
        first = offset + g
        columns = [
            jnp.broadcast_to(m[:, first + k : first + k + 1], (left, LANES))
            for k in range(GROUP)
        ]
        for k in range(GROUP):
            pivot = columns[k][k : k + 1, :]
            f = jnp.where(at > k, columns[k] * (1.0 / pivot), 0.0)
            for l in range(k + 1, GROUP):
                columns[l] = columns[l] - f * columns[l][k : k + 1, :]
            root = lax.rsqrt(pivot)
            root = root * (1.5 - 0.5 * pivot * root * root)
            done.append(e[k : k + 1, :] * root)
            m = m - f * m[k : k + 1, :]
            e = e - f * e[k : k + 1, :]
        m, e = m[GROUP:], e[GROUP:]
    return jnp.concatenate(done, axis=0)


def factorize(u_out, x_out, work):
    rank = work.shape[0]
    for r in range(0, rank, BLOCK):
        tile, offset = r // LANES * LANES, r % LANES
        x = eliminate(work[r : r + BLOCK, tile : tile + LANES], offset, BLOCK)
        line = dot3(split(x[:, :BLOCK]), split(work[r : r + BLOCK, :]))
        row = lax.broadcasted_iota(jnp.int32, (BLOCK, rank), 0) + r
        column = lax.broadcasted_iota(jnp.int32, (BLOCK, rank), 1)
        upper = jnp.where(column >= row, line[:, :rank], 0.0)
        u_out[r : r + BLOCK, :rank] = upper
        x_out[r : r + BLOCK, :] = line[:, rank:]
        if r + BLOCK < rank:
            below = slice(r + BLOCK, rank)
            work[below, :] = work[below, :] - dot3(split(upper.T[below, :]), split(line))


def unpack_gram(state, work):
    rank = work.shape[0]
    half = rank // 2
    a, b, c = gram_blocks(state)
    work[:half, :half] = a
    work[:half, half:rank] = b
    work[half:, :half] = jnp.zeros_like(b)
    work[half:, half:rank] = c
    rows = lax.broadcasted_iota(jnp.int32, (rank, rank), 0)
    columns = lax.broadcasted_iota(jnp.int32, (rank, rank), 1)
    work[:, rank:] = jnp.where(rows == columns, 1.0, 0.0).astype(F32)


def factor_own(section, *refs):
    *states, u_out, x_out, work = refs
    for k, state in enumerate(states):

        @pl.when(section[0] == k)
        def _(state=state):
            unpack_gram(state, work)

    @pl.when(section[0] < len(states))
    def _():
        factorize(u_out, x_out, work)


def factor_last(flags, state, beside, x_own, both, x_out, work):
    rank = work.shape[0]

    @pl.when(flags[0] == 0)
    def _():
        x_out[...] = x_own[...]

    @pl.when(flags[0] != 0)
    def _():
        first = flags[1] == 0
        link = whole_link(first, state[3 * rank // 2 :, :], beside[...])
        both[:, rank:] = jnp.where(first, link, link.T)
        unpack_gram(state, work)
        factorize(both, x_out, work)


def frame(scale, own, upper, inverse, out):
    u = split(upper[...])
    x = split(inverse[...] * scale)
    for i in range(own.shape[0]):
        mixed = split(dot3(u, split(own[i])))
        out[i] = dot3(mixed, x, ((1,), (1,)))


def swapped(x):
    return lax.ppermute(x, "tensor", [(0, 1), (1, 0)])


def scalars(*values):
    return jnp.stack([v.astype(jnp.int32) for v in values])


def shards(cores, incoming):
    own, up = cores[0, 0], incoming[0]
    modes, rank, _ = own.shape
    half = rank // 2
    section, which = lax.axis_index("cores"), lax.axis_index("tensor")
    sections, rows = lax.axis_size("cores"), lax.axis_size("row")
    last = sections - 1

    other, up_other = swapped(own), swapped(up)
    wide, narrow = ((rank, modes * rank), BF16), ((rank, modes * half), BF16)
    packed, side = ((3 * half + rank, half), F32), ((rank, half), F32)
    square = ((rank, rank), F32)
    scratch = [pltpu.VMEM((rank, 2 * rank), F32)]
    own_parts = call(prepare_own, [wide] * 4, [VMEM])(own)
    *link_parts, state, beside = call(
        prepare_link, [wide] * 2 + [narrow] * 2 + [packed, side], [SMEM] + [VMEM] * 6
    )(scalars(which), own, other, *own_parts[2:], up, up_other)
    run_chain = call(chain, [packed], [SMEM] + [VMEM] * 10)

    def exchange(x, pair):
        if pair is None:
            return lax.all_to_all(x, "row", 0, 0, tiled=True)
        rest = [k for k in range(sections) if k not in pair]
        groups = [[k * rows + r for k in p for r in range(rows)] for p in (pair, rest)]
        return lax.all_to_all(
            x, ("cores", "row"), 0, 0, tiled=True, axis_index_groups=groups
        )

    states = []
    for tick in range(sections):
        (partial,) = run_chain(scalars(which), state, beside, *own_parts, *link_parts)
        pair = (tick, tick + 1) if tick < last else None
        count = rows * (2 if pair else 1)
        arrived = exchange(partial.reshape(count, 1, -1), pair)
        piece = arrived[:rows].sum(axis=0)
        copies = jnp.broadcast_to(piece[None], arrived.shape)
        state = exchange(copies, pair).reshape(partial.shape)
        beside = swapped(state[3 * half :])
        states.append(state)
        if tick == last - 1:
            u_own, x_own = call(
                factor_own, [square] * 2, [SMEM] + [VMEM] * last, scratch
            )(scalars(section), *states)
            state, beside, u_own, x_own = lax.optimization_barrier(
                (state, beside, u_own, x_own)
            )
            u_before = lax.ppermute(u_own, "cores", [(k, k + 1) for k in range(last)])
            u_before = jnp.where(section == 0, up, u_before)

    both, x_own = call(
        factor_last, [((rank, 2 * rank), F32), square], [SMEM] + [VMEM] * 3, scratch
    )(scalars(section == last, which), state, beside, x_own)
    share = rank // sections
    tiles = both.reshape(sections, share, 2 * rank)
    sent = [lax.ppermute(tiles[k], "cores", [(last, k)]) for k in range(last)]
    (frames,) = call(
        functools.partial(frame, float(MODE * rank) ** 0.5), [(own.shape, F32)], [VMEM] * 3
    )(own, u_before, x_own)
    result = tiles[last]
    for k in range(last):
        result = jnp.where(section == k, sent[k], result)
    return frames[None, None], result[None, :, :rank], result[None, :, rank:]


def solution(mesh):
    in_specs = (P("tensor", "cores", "row", None, None), P("tensor", None, None))
    out_specs = (
        P("tensor", "cores", "row", None, None),
        P("tensor", "cores", None),
        P("tensor", "cores", None),
    )
    return jax.shard_map(shards, mesh=mesh, in_specs=in_specs, out_specs=out_specs, check_vma=False)
```

```python
import functools

import jax
import jax.numpy as jnp
from jax import lax
from jax.experimental import pallas as pl
from jax.experimental.pallas import tpu as pltpu
from jax.sharding import PartitionSpec as P

MODE = 128
LANES = 128
BLOCK = 64
GROUP = 8
VMEM_LIMIT = 16 * 1024 * 1024
F32 = jnp.float32
BF16 = jnp.bfloat16

VMEM = pl.BlockSpec(memory_space=pltpu.VMEM)
SMEM = pl.BlockSpec(memory_space=pltpu.SMEM)
HBM = pl.BlockSpec(memory_space=pltpu.HBM)


def call(body, outs, in_specs, scratch=(), out_spec=VMEM):
    return pl.pallas_call(
        body,
        out_shape=[jax.ShapeDtypeStruct(s, d) for s, d in outs],
        in_specs=in_specs,
        out_specs=[out_spec] * len(outs),
        scratch_shapes=list(scratch),
        compiler_params=pltpu.CompilerParams(vmem_limit_bytes=VMEM_LIMIT),
    )


def split(x):
    hi = x.astype(BF16)
    return hi, (x - hi.astype(F32)).astype(BF16)


def dot(a, b, dims=((1,), (0,))):
    return lax.dot_general(a, b, (dims, ((), ())), preferred_element_type=F32)


def dot3(a, b, dims=((1,), (0,))):
    (ah, al), (bh, bl) = a, b
    return dot(ah, bh, dims) + (dot(ah, bl, dims) + dot(al, bh, dims))


def full(a, b, dims=((1,), (0,))):
    return lax.dot_general(
        a, b, (dims, ((), ())), precision=lax.Precision.HIGHEST, preferred_element_type=F32
    )


def pack_gram(out, gram):
    half = gram.shape[0] // 2
    out[0:half, :] = gram[:half, :half]
    out[half : 2 * half, :] = gram[:half, half:]
    out[2 * half : 3 * half, :] = gram[half:, half:]


def gram_blocks(state):
    half = LANES
    return state[0:half, :], state[half : 2 * half, :], state[2 * half : 3 * half, :]


def whole_link(first, mine, theirs):
    return jnp.concatenate(
        [jnp.where(first, mine, theirs), jnp.where(first, theirs, mine)], axis=1
    )


def prepare_own(own, ch, cl, th, tl):
    modes, rank = own.shape[0], own.shape[1]
    for i in range(modes):
        at = pl.ds(i * rank, rank)
        mine = own[i]
        ch[:, at], cl[:, at] = split(mine)
        th[:, at], tl[:, at] = split(mine.T)


def prepare_link(which, own, other, th, tl, up, up_other, lh, ll, rh, rl, start, beside):
    modes, rank = own.shape[0], own.shape[1]
    half = rank // 2
    u, v = up[...], up_other[...]
    pack_gram(start, full(u, u, ((0,), (0,))))

    def sides(left, right, mine, theirs):
        link = full(left, right, ((0,), (0,)))
        start[3 * half :, :] = link[:, mine]
        beside[...] = link[:, theirs]

    low, high = slice(0, half), slice(half, rank)

    @pl.when(which[0] == 0)
    def _():
        lh[...] = th[...]
        ll[...] = tl[...]
        for i in range(modes):
            at = pl.ds(i * half, half)
            rh[:, at], rl[:, at] = split(other[i][:, low])
        sides(u, v, low, high)

    @pl.when(which[0] != 0)
    def _():
        for i in range(modes):
            at = pl.ds(i * half, half)
            rh[:, at], rl[:, at] = split(own[i][:, high])
            at = pl.ds(i * rank, rank)
            lh[:, at], ll[:, at] = split(other[i].T)
        sides(v, u, high, low)


def stacked(x, width):
    return jnp.concatenate(
        [x[:, i : i + width] for i in range(0, x.shape[1], width)], axis=0
    )


def chain_product(middle, right, left, width):
    mh, ml = split(dot3(middle, right))
    return dot3(left, (stacked(mh, width), stacked(ml, width)))


def chain_gram(state, ch, cl, th, tl, out):
    rank = ch.shape[0]
    a, b, c = gram_blocks(state)
    gram = jnp.concatenate(
        [jnp.concatenate([a, b], axis=1), jnp.concatenate([b.T, c], axis=1)], axis=0
    )
    pack_gram(out, chain_product(split(gram), (ch[...], cl[...]), (th[...], tl[...]), rank))


def chain_gram_keep(tick, section, kept, state, ch, cl, th, tl, out, keep):
    mine = section[0] == tick - 1
    keep[...] = jnp.where(mine, state[: keep.shape[0], :], kept[...])
    chain_gram(state, ch, cl, th, tl, out)


def chain_link(which, gram, state, beside, lh, ll, rh, rl, out):
    rank = lh.shape[0]
    half = rank // 2
    out[: 3 * half, :] = gram[...]
    link = whole_link(which[0] == 0, state[3 * half :, :], beside[...])
    out[3 * half :, :] = chain_product(
        split(link), (rh[...], rl[...]), (lh[...], ll[...]), half
    )


def eliminate(m, offset, n):
    rows = lax.broadcasted_iota(jnp.int32, (n, LANES), 0)
    lanes = lax.broadcasted_iota(jnp.int32, (n, LANES), 1)
    e = jnp.where(rows == lanes, 1.0, 0.0).astype(F32)
    done = []
    for g in range(0, n, GROUP):
        left = n - g
        at = lax.broadcasted_iota(jnp.int32, (left, LANES), 0)
        first = offset + g
        columns = [
            jnp.broadcast_to(m[:, first + k : first + k + 1], (left, LANES))
            for k in range(GROUP)
        ]
        for k in range(GROUP):
            pivot = columns[k][k : k + 1, :]
            f = jnp.where(at > k, columns[k] * (1.0 / pivot), 0.0)
            for l in range(k + 1, GROUP):
                columns[l] = columns[l] - f * columns[l][k : k + 1, :]
            root = lax.rsqrt(pivot)
            root = root * (1.5 - 0.5 * pivot * root * root)
            done.append(e[k : k + 1, :] * root)
            m = m - f * m[k : k + 1, :]
            e = e - f * e[k : k + 1, :]
        m, e = m[GROUP:], e[GROUP:]
    return jnp.concatenate(done, axis=0)


def factorize(u_out, x_out, work):
    rank = work.shape[0]
    for r in range(0, rank, BLOCK):
        tile, offset = r // LANES * LANES, r % LANES
        x = eliminate(work[r : r + BLOCK, tile : tile + LANES], offset, BLOCK)
        line = dot3(split(x[:, :BLOCK]), split(work[r : r + BLOCK, :]))
        row = lax.broadcasted_iota(jnp.int32, (BLOCK, rank), 0) + r
        column = lax.broadcasted_iota(jnp.int32, (BLOCK, rank), 1)
        upper = jnp.where(column >= row, line[:, :rank], 0.0)
        u_out[r : r + BLOCK, :rank] = upper
        x_out[r : r + BLOCK, :] = line[:, rank:]
        if r + BLOCK < rank:
            below = slice(r + BLOCK, rank)
            work[below, :] = work[below, :] - dot3(split(upper.T[below, :]), split(line))


def unpack_gram(state, work):
    rank = work.shape[0]
    half = rank // 2
    a, b, c = gram_blocks(state)
    work[:half, :half] = a
    work[:half, half:rank] = b
    work[half:, :half] = jnp.zeros_like(b)
    work[half:, half:rank] = c
    rows = lax.broadcasted_iota(jnp.int32, (rank, rank), 0)
    columns = lax.broadcasted_iota(jnp.int32, (rank, rank), 1)
    work[:, rank:] = jnp.where(rows == columns, 1.0, 0.0).astype(F32)


def factor_own(section, kept, state, u_out, x_out, work, gram, u, x):
    busy = section[0] < section[1]

    @pl.when(busy)
    def _():
        pltpu.sync_copy(kept, gram)

    @pl.when(section[0] == section[1] - 1)
    def _():
        pltpu.sync_copy(state.at[pl.ds(0, gram.shape[0])], gram)

    @pl.when(busy)
    def _():
        unpack_gram(gram, work)
        factorize(u, x, work)
        pltpu.sync_copy(u, u_out)
        pltpu.sync_copy(x, x_out)


def factor_last(place, state, beside, x_own, tail, correlation, x_out, work, square):
    rank = work.shape[0]
    rows = pl.ds(pl.multiple_of(place[0] * tail.shape[0], tail.shape[0]), tail.shape[0])
    first = place[1] == 0
    link = whole_link(first, state[3 * rank // 2 :, :], beside[...])
    square[...] = jnp.where(first, link, link.T)
    correlation[...] = square[rows, :]
    unpack_gram(state, work)
    factorize(square, x_out, work)
    tail[...] = square[rows, :]

    @pl.when(place[2] == 0)
    def _():
        x_out[...] = x_own[...]


def frame(scale, own, upper, inverse, out):
    u = split(upper[...])
    x = split(inverse[...] * scale)
    for i in range(own.shape[0]):
        mixed = split(dot3(u, split(own[i])))
        out[i] = dot3(mixed, x, ((1,), (1,)))


def swapped(x):
    return lax.ppermute(x, "tensor", [(0, 1), (1, 0)])


def scalars(*values):
    return jnp.stack([jnp.asarray(v, jnp.int32) for v in values])


def shards(cores, incoming):
    own, up = cores[0, 0], incoming[0]
    modes, rank, _ = own.shape
    half = rank // 2
    section, which = lax.axis_index("cores"), lax.axis_index("tensor")
    sections, rows = lax.axis_size("cores"), lax.axis_size("row")
    last = sections - 1

    other, up_other = swapped(own), swapped(up)
    wide, narrow = ((rank, modes * rank), BF16), ((rank, modes * half), BF16)
    packed, side = ((3 * half + rank, half), F32), ((rank, half), F32)
    square = ((rank, rank), F32)
    scratch = [pltpu.VMEM((rank, 2 * rank), F32)]
    own_parts = call(prepare_own, [wide] * 4, [VMEM])(own)
    *link_parts, state, beside = call(
        prepare_link, [wide] * 2 + [narrow] * 2 + [packed, side], [SMEM] + [VMEM] * 6
    )(scalars(which), own, other, *own_parts[2:], up, up_other)
    gram_shape = ((3 * half, half), F32)
    run_gram = call(chain_gram, [gram_shape], [VMEM] * 5)
    run_link = call(chain_link, [packed], [SMEM] + [VMEM] * 7)

    def exchange(x, pair):
        if pair is None:
            return lax.all_to_all(x, "row", 0, 0, tiled=True)
        rest = [k for k in range(sections) if k not in pair]
        groups = [[k * rows + r for k in p for r in range(rows)] for p in (pair, rest)]
        return lax.all_to_all(
            x, ("cores", "row"), 0, 0, tiled=True, axis_index_groups=groups
        )

    kept = None
    for tick in range(sections):
        if 0 < tick < last:
            gram, kept = call(
                functools.partial(chain_gram_keep, tick),
                [gram_shape] * 2,
                [SMEM] + [VMEM] * 6,
            )(scalars(section), kept, state, *own_parts)
        else:
            (gram,) = run_gram(state, *own_parts)
            kept = gram if tick == 0 else kept
        (partial,) = run_link(scalars(which), gram, state, beside, *link_parts)
        pair = (tick, tick + 1) if tick < last else None
        count = rows * (2 if pair else 1)
        arrived = exchange(partial.reshape(count, 1, -1), pair)
        piece = arrived[:rows].sum(axis=0)
        if tick == last:
            sent = [lax.ppermute(piece, "cores", [(last, k)]) for k in range(last)]
            for k in range(last):
                piece = jnp.where(section == k, sent[k], piece)
        copies = jnp.broadcast_to(piece[None], arrived.shape)
        state = exchange(copies, pair).reshape(partial.shape)
        beside = swapped(state[3 * half :])
        if tick == last - 1:
            u_own, x_own = call(
                factor_own,
                [square] * 2,
                [SMEM] + [HBM] * 2,
                scratch + [pltpu.VMEM(*gram_shape)] + [pltpu.VMEM(*square)] * 2,
                HBM,
            )(scalars(section, last), kept, state)
            state, u_own, x_own = lax.optimization_barrier((state, u_own, x_own))
            u_before = lax.ppermute(u_own, "cores", [(k, k + 1) for k in range(last)])
            u_before = jnp.where(section == 0, up, u_before)

    share = ((rank // sections, rank), F32)
    tail, correlation, x_own = call(
        factor_last,
        [share, share, square],
        [SMEM] + [VMEM] * 3,
        scratch + [pltpu.VMEM((rank, rank), F32)],
    )(scalars(section, which, section == last), state, beside, x_own)
    (frames,) = call(
        functools.partial(frame, float(MODE * rank) ** 0.5), [(own.shape, F32)], [VMEM] * 3
    )(own, u_before, x_own)
    return frames[None, None], tail[None], correlation[None]


def solution(mesh):
    in_specs = (P("tensor", "cores", "row", None, None), P("tensor", None, None))
    out_specs = (
        P("tensor", "cores", "row", None, None),
        P("tensor", "cores", None),
        P("tensor", "cores", None),
    )
    return jax.shard_map(shards, mesh=mesh, in_specs=in_specs, out_specs=out_specs, check_vma=False)
```

```python
import functools

import jax
import jax.numpy as jnp
from jax import lax
from jax.experimental import pallas as pl
from jax.experimental.pallas import tpu as pltpu
from jax.sharding import PartitionSpec as P

MODE = 128
LANES = 128
BLOCK = 64
GROUP = 8
VMEM_LIMIT = 16 * 1024 * 1024
F32 = jnp.float32
BF16 = jnp.bfloat16

VMEM = pl.BlockSpec(memory_space=pltpu.VMEM)
SMEM = pl.BlockSpec(memory_space=pltpu.SMEM)
HBM = pl.BlockSpec(memory_space=pltpu.HBM)


def call(body, outs, in_specs, scratch=(), out_spec=VMEM):
    return pl.pallas_call(
        body,
        out_shape=[jax.ShapeDtypeStruct(s, d) for s, d in outs],
        in_specs=in_specs,
        out_specs=[out_spec] * len(outs),
        scratch_shapes=list(scratch),
        compiler_params=pltpu.CompilerParams(vmem_limit_bytes=VMEM_LIMIT),
    )


def split(x):
    hi = x.astype(BF16)
    return hi, (x - hi.astype(F32)).astype(BF16)


def dot(a, b, dims=((1,), (0,))):
    return lax.dot_general(a, b, (dims, ((), ())), preferred_element_type=F32)


def dot3(a, b, dims=((1,), (0,))):
    (ah, al), (bh, bl) = a, b
    return dot(ah, bh, dims) + (dot(ah, bl, dims) + dot(al, bh, dims))


def full(a, b, dims=((1,), (0,))):
    return lax.dot_general(
        a, b, (dims, ((), ())), precision=lax.Precision.HIGHEST, preferred_element_type=F32
    )


def pack_gram(out, gram):
    half = gram.shape[0] // 2
    out[0:half, :] = gram[:half, :half]
    out[half : 2 * half, :] = gram[:half, half:]
    out[2 * half : 3 * half, :] = gram[half:, half:]


def gram_blocks(state):
    half = LANES
    return state[0:half, :], state[half : 2 * half, :], state[2 * half : 3 * half, :]


def whole_link(first, mine, theirs):
    return jnp.concatenate(
        [jnp.where(first, mine, theirs), jnp.where(first, theirs, mine)], axis=1
    )


def prepare_own(own, ch, cl, th, tl):
    modes, rank = own.shape[0], own.shape[1]
    for i in range(modes):
        at = pl.ds(i * rank, rank)
        mine = own[i]
        ch[:, at], cl[:, at] = split(mine)
        th[:, at], tl[:, at] = split(mine.T)


def prepare_link(which, own, other, th, tl, up, up_other, lh, ll, rh, rl, start, beside):
    modes, rank = own.shape[0], own.shape[1]
    half = rank // 2
    u, v = up[...], up_other[...]
    pack_gram(start, full(u, u, ((0,), (0,))))

    def sides(left, right, mine, theirs):
        link = full(left, right, ((0,), (0,)))
        start[3 * half :, :] = link[:, mine]
        beside[...] = link[:, theirs]

    low, high = slice(0, half), slice(half, rank)

    @pl.when(which[0] == 0)
    def _():
        lh[...] = th[...]
        ll[...] = tl[...]
        for i in range(modes):
            at = pl.ds(i * half, half)
            rh[:, at], rl[:, at] = split(other[i][:, low])
        sides(u, v, low, high)

    @pl.when(which[0] != 0)
    def _():
        for i in range(modes):
            at = pl.ds(i * half, half)
            rh[:, at], rl[:, at] = split(own[i][:, high])
            at = pl.ds(i * rank, rank)
            lh[:, at], ll[:, at] = split(other[i].T)
        sides(v, u, high, low)


def stacked(x, width):
    return jnp.concatenate(
        [x[:, i : i + width] for i in range(0, x.shape[1], width)], axis=0
    )


def chain_product(middle, right, left, width):
    mh, ml = split(dot3(middle, right))
    return dot3(left, (stacked(mh, width), stacked(ml, width)))


def chain_gram(tick, place, state, ch, cl, th, tl, out):
    rank = ch.shape[0]

    @pl.when(place[0] == tick)
    def _():
        a, b, c = gram_blocks(state)
        gram = jnp.concatenate(
            [jnp.concatenate([a, b], axis=1), jnp.concatenate([b.T, c], axis=1)], axis=0
        )
        pack_gram(
            out, chain_product(split(gram), (ch[...], cl[...]), (th[...], tl[...]), rank)
        )


def chain_gram_keep(tick, place, kept, state, ch, cl, th, tl, out, keep):
    mine = place[0] == tick - 1
    keep[...] = jnp.where(mine, state[: keep.shape[0], :], kept[...])
    chain_gram(tick, place, state, ch, cl, th, tl, out)


def chain_link(tick, place, gram, state, beside, lh, ll, rh, rl, out):
    rank = lh.shape[0]
    half = rank // 2

    @pl.when(place[0] == tick)
    def _():
        out[: 3 * half, :] = gram[...]
        link = whole_link(place[1] == 0, state[3 * half :, :], beside[...])
        out[3 * half :, :] = chain_product(
            split(link), (rh[...], rl[...]), (lh[...], ll[...]), half
        )


def eliminate(m, offset, n):
    rows = lax.broadcasted_iota(jnp.int32, (n, LANES), 0)
    lanes = lax.broadcasted_iota(jnp.int32, (n, LANES), 1)
    e = jnp.where(rows == lanes, 1.0, 0.0).astype(F32)
    done = []
    for g in range(0, n, GROUP):
        left = n - g
        at = lax.broadcasted_iota(jnp.int32, (left, LANES), 0)
        first = offset + g
        columns = [
            jnp.broadcast_to(m[:, first + k : first + k + 1], (left, LANES))
            for k in range(GROUP)
        ]
        for k in range(GROUP):
            pivot = columns[k][k : k + 1, :]
            f = jnp.where(at > k, columns[k] * (1.0 / pivot), 0.0)
            for l in range(k + 1, GROUP):
                columns[l] = columns[l] - f * columns[l][k : k + 1, :]
            root = lax.rsqrt(pivot)
            root = root * (1.5 - 0.5 * pivot * root * root)
            done.append(e[k : k + 1, :] * root)
            m = m - f * m[k : k + 1, :]
            e = e - f * e[k : k + 1, :]
        m, e = m[GROUP:], e[GROUP:]
    return jnp.concatenate(done, axis=0)


def factorize(u_out, x_out, work):
    rank = work.shape[0]
    for r in range(0, rank, BLOCK):
        tile, offset = r // LANES * LANES, r % LANES
        x = eliminate(work[r : r + BLOCK, tile : tile + LANES], offset, BLOCK)
        line = dot3(split(x[:, :BLOCK]), split(work[r : r + BLOCK, :]))
        row = lax.broadcasted_iota(jnp.int32, (BLOCK, rank), 0) + r
        column = lax.broadcasted_iota(jnp.int32, (BLOCK, rank), 1)
        upper = jnp.where(column >= row, line[:, :rank], 0.0)
        u_out[r : r + BLOCK, :rank] = upper
        x_out[r : r + BLOCK, :] = line[:, rank:]
        if r + BLOCK < rank:
            below = slice(r + BLOCK, rank)
            work[below, :] = work[below, :] - dot3(split(upper.T[below, :]), split(line))


def unpack_gram(state, work):
    rank = work.shape[0]
    half = rank // 2
    a, b, c = gram_blocks(state)
    work[:half, :half] = a
    work[:half, half:rank] = b
    work[half:, :half] = jnp.zeros_like(b)
    work[half:, half:rank] = c
    rows = lax.broadcasted_iota(jnp.int32, (rank, rank), 0)
    columns = lax.broadcasted_iota(jnp.int32, (rank, rank), 1)
    work[:, rank:] = jnp.where(rows == columns, 1.0, 0.0).astype(F32)


def factor_own(section, kept, state, u_out, x_out, work, gram, u, x):
    busy = section[0] < section[1]

    @pl.when(busy)
    def _():
        pltpu.sync_copy(kept, gram)

    @pl.when(section[0] == section[1] - 1)
    def _():
        pltpu.sync_copy(state.at[pl.ds(0, gram.shape[0])], gram)

    @pl.when(busy)
    def _():
        unpack_gram(gram, work)
        factorize(u, x, work)
        pltpu.sync_copy(u, u_out)
        pltpu.sync_copy(x, x_out)


def factor_last(flags, state, beside, x_own, both, x_out, work):
    rank = work.shape[0]

    @pl.when(flags[0] == 0)
    def _():
        x_out[...] = x_own[...]

    @pl.when(flags[0] != 0)
    def _():
        first = flags[1] == 0
        link = whole_link(first, state[3 * rank // 2 :, :], beside[...])
        both[:, rank:] = jnp.where(first, link, link.T)
        unpack_gram(state, work)
        factorize(both, x_out, work)


def frame(scale, own, upper, inverse, out):
    u = split(upper[...])
    x = split(inverse[...] * scale)
    for i in range(own.shape[0]):
        mixed = split(dot3(u, split(own[i])))
        out[i] = dot3(mixed, x, ((1,), (1,)))


def swapped(x):
    return lax.ppermute(x, "tensor", [(0, 1), (1, 0)])


def scalars(*values):
    return jnp.stack([jnp.asarray(v, jnp.int32) for v in values])


def shards(cores, incoming):
    own, up = cores[0, 0], incoming[0]
    modes, rank, _ = own.shape
    half = rank // 2
    section, which = lax.axis_index("cores"), lax.axis_index("tensor")
    sections, rows = lax.axis_size("cores"), lax.axis_size("row")
    last = sections - 1

    other, up_other = swapped(own), swapped(up)
    wide, narrow = ((rank, modes * rank), BF16), ((rank, modes * half), BF16)
    packed, side = ((3 * half + rank, half), F32), ((rank, half), F32)
    square = ((rank, rank), F32)
    scratch = [pltpu.VMEM((rank, 2 * rank), F32)]
    own_parts = call(prepare_own, [wide] * 4, [VMEM])(own)
    *link_parts, state, beside = call(
        prepare_link, [wide] * 2 + [narrow] * 2 + [packed, side], [SMEM] + [VMEM] * 6
    )(scalars(which), own, other, *own_parts[2:], up, up_other)
    gram_shape = ((3 * half, half), F32)
    near = max(1, rows // 4)
    far = rows // near
    place = scalars(section, which)

    def exchange(x, pair):
        blocks = [[g * near + j for j in range(near)] for g in range(far)]
        if pair is None:
            return lax.all_to_all(x, "row", 0, 0, tiled=True, axis_index_groups=blocks)
        rest = [k for k in range(sections) if k not in pair]
        groups = [[k * rows + r for k in p for r in b] for p in (pair, rest) for b in blocks]
        return lax.all_to_all(
            x, ("cores", "row"), 0, 0, tiled=True, axis_index_groups=groups
        )

    def over_far(x):
        terms = [x]
        for step in range(1, far):
            pairs = [(r, (r + step * near) % rows) for r in range(rows)]
            terms.append(lax.ppermute(x, "row", pairs))
        return sum(terms[2::2], terms[0]) + sum(terms[3::2], terms[1])

    kept = None
    for tick in range(sections):
        if 0 < tick < last:
            gram, kept = call(
                functools.partial(chain_gram_keep, tick),
                [gram_shape] * 2,
                [SMEM] + [VMEM] * 6,
            )(place, kept, state, *own_parts)
        else:
            (gram,) = call(
                functools.partial(chain_gram, tick), [gram_shape], [SMEM] + [VMEM] * 5
            )(place, state, *own_parts)
            kept = gram if tick == 0 else kept
        (partial,) = call(
            functools.partial(chain_link, tick), [packed], [SMEM] + [VMEM] * 7
        )(place, gram, state, beside, *link_parts)
        pair = (tick, tick + 1) if tick < last else None
        count = near * (2 if pair else 1)
        arrived = exchange(partial.reshape(count, -1, half), pair)
        piece = over_far(arrived[:near].sum(axis=0))
        copies = jnp.broadcast_to(piece[None], arrived.shape)
        state = exchange(copies, pair).reshape(partial.shape)
        beside = swapped(state[3 * half :])
        if tick == last - 1:
            u_own, x_own = call(
                factor_own,
                [square] * 2,
                [SMEM] + [HBM] * 2,
                scratch + [pltpu.VMEM(*gram_shape)] + [pltpu.VMEM(*square)] * 2,
                HBM,
            )(scalars(section, last), kept, state)
            state, u_own, x_own = lax.optimization_barrier((state, u_own, x_own))
            u_before = lax.ppermute(u_own, "cores", [(k, k + 1) for k in range(last)])
            u_before = jnp.where(section == 0, up, u_before)

    both, x_own = call(
        factor_last, [((rank, 2 * rank), F32), square], [SMEM] + [VMEM] * 3, scratch
    )(scalars(section == last, which), state, beside, x_own)
    share = rank // sections
    tiles = both.reshape(sections, share, 2 * rank)
    sent = [lax.ppermute(tiles[k], "cores", [(last, k)]) for k in range(last)]
    (frames,) = call(
        functools.partial(frame, float(MODE * rank) ** 0.5), [(own.shape, F32)], [VMEM] * 3
    )(own, u_before, x_own)
    result = tiles[last]
    for k in range(last):
        result = jnp.where(section == k, sent[k], result)
    return frames[None, None], result[None, :, :rank], result[None, :, rank:]


def solution(mesh):
    in_specs = (P("tensor", "cores", "row", None, None), P("tensor", None, None))
    out_specs = (
        P("tensor", "cores", "row", None, None),
        P("tensor", "cores", None),
        P("tensor", "cores", None),
    )
    return jax.shard_map(shards, mesh=mesh, in_specs=in_specs, out_specs=out_specs, check_vma=False)
```

```python
import functools

import jax
import jax.numpy as jnp
from jax import lax
from jax.experimental import pallas as pl
from jax.experimental.pallas import tpu as pltpu
from jax.sharding import PartitionSpec as P

MODE = 128
LANES = 128
BLOCK = 64
GROUP = 16
VMEM_LIMIT = 16 * 1024 * 1024
F32 = jnp.float32
BF16 = jnp.bfloat16

VMEM = pl.BlockSpec(memory_space=pltpu.VMEM)
SMEM = pl.BlockSpec(memory_space=pltpu.SMEM)
HBM = pl.BlockSpec(memory_space=pltpu.HBM)


def call(body, outs, in_specs, scratch=(), out_spec=VMEM):
    return pl.pallas_call(
        body,
        out_shape=[jax.ShapeDtypeStruct(s, d) for s, d in outs],
        in_specs=in_specs,
        out_specs=[out_spec] * len(outs),
        scratch_shapes=list(scratch),
        compiler_params=pltpu.CompilerParams(vmem_limit_bytes=VMEM_LIMIT),
    )


def split(x):
    hi = x.astype(BF16)
    return hi, (x - hi.astype(F32)).astype(BF16)


def dot(a, b, dims=((1,), (0,))):
    return lax.dot_general(a, b, (dims, ((), ())), preferred_element_type=F32)


def dot3(a, b, dims=((1,), (0,))):
    (ah, al), (bh, bl) = a, b
    return dot(ah, bh, dims) + (dot(ah, bl, dims) + dot(al, bh, dims))


def pack_gram(out, gram):
    half = gram.shape[0] // 2
    out[0:half, :] = gram[:half, :half]
    out[half : 2 * half, :] = gram[:half, half:]
    out[2 * half : 3 * half, :] = gram[half:, half:]


def gram_blocks(state):
    half = LANES
    return state[0:half, :], state[half : 2 * half, :], state[2 * half : 3 * half, :]


def whole_link(first, mine, theirs):
    return jnp.concatenate(
        [jnp.where(first, mine, theirs), jnp.where(first, theirs, mine)], axis=1
    )


def prepare_own(own, up, ch, cl, th, tl, start):
    modes, rank = own.shape[0], own.shape[1]
    u = split(up[...].T)
    pack_gram(start, dot3(u, u, ((1,), (1,))))
    for i in range(modes):
        at = pl.ds(i * rank, rank)
        mine = own[i]
        ch[:, at], cl[:, at] = split(mine)
        th[:, at], tl[:, at] = split(mine.T)


def prepare_link(which, own, other, th, tl, up, up_other, lh, ll, rh, rl, start, beside):
    modes, rank = own.shape[0], own.shape[1]
    half = rank // 2

    def sides(left, right, mine, theirs):
        link = dot3(split(left.T), split(right))
        start[...] = link[:, mine]
        beside[...] = link[:, theirs]

    low, high = slice(0, half), slice(half, rank)

    @pl.when(which[0] == 0)
    def _():
        lh[...] = th[...]
        ll[...] = tl[...]
        for i in range(modes):
            at = pl.ds(i * half, half)
            rh[:, at], rl[:, at] = split(other[i][:, low])
        sides(up[...], up_other[...], low, high)

    @pl.when(which[0] != 0)
    def _():
        for i in range(modes):
            at = pl.ds(i * half, half)
            rh[:, at], rl[:, at] = split(own[i][:, high])
            at = pl.ds(i * rank, rank)
            lh[:, at], ll[:, at] = split(other[i].T)
        sides(up_other[...], up[...], high, low)


def stacked(x, width):
    return jnp.concatenate(
        [x[:, i : i + width] for i in range(0, x.shape[1], width)], axis=0
    )


def chain_product(middle, right, left, width):
    mh, ml = split(dot3(middle, right))
    return dot3(left, (stacked(mh, width), stacked(ml, width)))


def chain_gram(state, ch, cl, th, tl, out):
    rank = ch.shape[0]
    a, b, c = gram_blocks(state)
    gram = jnp.concatenate(
        [jnp.concatenate([a, b], axis=1), jnp.concatenate([b.T, c], axis=1)], axis=0
    )
    pack_gram(out, chain_product(split(gram), (ch[...], cl[...]), (th[...], tl[...]), rank))


def chain_gram_keep(tick, place, kept, state, ch, cl, th, tl, out, keep):
    mine = place[0] == tick - 1
    keep[...] = jnp.where(mine, state[: keep.shape[0], :], kept[...])
    chain_gram(state, ch, cl, th, tl, out)


def chain_gram_last(tick, place, *refs):
    @pl.when(place[0] == tick)
    def _():
        chain_gram(*refs)


def chain_link(place, gram, state, beside, lh, ll, rh, rl, out):
    rank = lh.shape[0]
    half = rank // 2
    out[: 3 * half, :] = gram[...]
    link = whole_link(place[1] == 0, state[state.shape[0] - rank :, :], beside[...])
    out[3 * half :, :] = chain_product(
        split(link), (rh[...], rl[...]), (lh[...], ll[...]), half
    )


def chain_link_last(tick, place, *refs):
    @pl.when(place[0] == tick)
    def _():
        chain_link(place, *refs)


def eliminate(m, offset, n):
    rows = lax.broadcasted_iota(jnp.int32, (n, LANES), 0)
    lanes = lax.broadcasted_iota(jnp.int32, (n, LANES), 1)
    e = jnp.where(rows == lanes, 1.0, 0.0).astype(F32)
    done = []
    for g in range(0, n, GROUP):
        left = n - g
        at = lax.broadcasted_iota(jnp.int32, (left, LANES), 0)
        first = offset + g
        columns = [
            jnp.broadcast_to(m[:, first + k : first + k + 1], (left, LANES))
            for k in range(GROUP)
        ]
        for k in range(GROUP):
            pivot = columns[k][k : k + 1, :]
            f = jnp.where(at > k, columns[k] * (1.0 / pivot), 0.0)
            for l in range(k + 1, GROUP):
                columns[l] = columns[l] - f * columns[l][k : k + 1, :]
            root = lax.rsqrt(pivot)
            root = root * (1.5 - 0.5 * pivot * root * root)
            done.append(e[k : k + 1, :] * root)
            m = m - f * m[k : k + 1, :]
            e = e - f * e[k : k + 1, :]
        m, e = m[GROUP:], e[GROUP:]
    return jnp.concatenate(done, axis=0)


def factorize(u_out, x_out, work):
    rank = work.shape[0]
    for r in range(0, rank, BLOCK):
        tile, offset = r // LANES * LANES, r % LANES
        x = eliminate(work[r : r + BLOCK, tile : tile + LANES], offset, BLOCK)
        line = dot3(split(x[:, :BLOCK]), split(work[r : r + BLOCK, :]))
        row = lax.broadcasted_iota(jnp.int32, (BLOCK, rank), 0) + r
        column = lax.broadcasted_iota(jnp.int32, (BLOCK, rank), 1)
        upper = jnp.where(column >= row, line[:, :rank], 0.0)
        u_out[r : r + BLOCK, :rank] = upper
        x_out[r : r + BLOCK, :] = line[:, rank:]
        if r + BLOCK < rank:
            below = slice(r + BLOCK, rank)
            work[below, :] = work[below, :] - dot3(split(upper.T[below, :]), split(line))


def unpack_gram(state, work):
    rank = work.shape[0]
    half = rank // 2
    a, b, c = gram_blocks(state)
    work[:half, :half] = a
    work[:half, half:rank] = b
    work[half:, :half] = jnp.zeros_like(b)
    work[half:, half:rank] = c
    rows = lax.broadcasted_iota(jnp.int32, (rank, rank), 0)
    columns = lax.broadcasted_iota(jnp.int32, (rank, rank), 1)
    work[:, rank:] = jnp.where(rows == columns, 1.0, 0.0).astype(F32)


def factor_own(section, kept, state, u_out, x_out, work, gram, u, x):
    busy = section[0] < section[1]

    @pl.when(busy)
    def _():
        pltpu.sync_copy(kept, gram)

    @pl.when(section[0] == section[1] - 1)
    def _():
        pltpu.sync_copy(state.at[pl.ds(0, gram.shape[0])], gram)

    @pl.when(busy)
    def _():
        unpack_gram(gram, work)
        factorize(u, x, work)
        pltpu.sync_copy(u, u_out)
        pltpu.sync_copy(x, x_out)


def factor_last(flags, state, beside, x_own, both, x_out, work):
    rank = work.shape[0]

    @pl.when(flags[0] == 0)
    def _():
        x_out[...] = x_own[...]

    @pl.when(flags[0] != 0)
    def _():
        first = flags[1] == 0
        link = whole_link(first, state[3 * rank // 2 :, :], beside[...])
        both[:, rank:] = jnp.where(first, link, link.T)
        unpack_gram(state, work)
        factorize(both, x_out, work)


def frame(scale, own, upper, inverse, out):
    u = split(upper[...])
    x = split(inverse[...] * scale)
    for i in range(own.shape[0]):
        mixed = split(dot3(u, split(own[i])))
        out[i] = dot3(mixed, x, ((1,), (1,)))


def swapped(x):
    return lax.ppermute(x, "tensor", [(0, 1), (1, 0)])


def scalars(*values):
    return jnp.stack([jnp.asarray(v, jnp.int32) for v in values])


def shards(cores, incoming):
    own, up = cores[0, 0], incoming[0]
    modes, rank, _ = own.shape
    half = rank // 2
    section, which = lax.axis_index("cores"), lax.axis_index("tensor")
    sections, rows = lax.axis_size("cores"), lax.axis_size("row")
    last = sections - 1

    other, up_other = swapped(own), swapped(up)
    wide, narrow = ((rank, modes * rank), BF16), ((rank, modes * half), BF16)
    packed, side = ((3 * half + rank, half), F32), ((rank, half), F32)
    square = ((rank, rank), F32)
    scratch = [pltpu.VMEM((rank, 2 * rank), F32)]
    gram_shape = ((3 * half, half), F32)
    *own_parts, state = call(prepare_own, [wide] * 4 + [gram_shape], [VMEM] * 2)(own, up)
    *link_parts, link, beside = call(
        prepare_link, [wide] * 2 + [narrow] * 2 + [side] * 2, [SMEM] + [VMEM] * 6
    )(scalars(which), own, other, *own_parts[2:], up, up_other)
    near = max(1, rows // 4)
    far = rows // near
    place = scalars(section, which)

    def exchange(x, pair):
        blocks = [[g * near + j for j in range(near)] for g in range(far)]
        if pair is None:
            return lax.all_to_all(x, "row", 0, 0, tiled=True, axis_index_groups=blocks)
        rest = [k for k in range(sections) if k not in pair]
        groups = [[k * rows + r for k in p for r in b] for p in (pair, rest) for b in blocks]
        return lax.all_to_all(
            x, ("cores", "row"), 0, 0, tiled=True, axis_index_groups=groups
        )

    def over_far(x):
        for step in (1, far - 1) if far > 2 else (1,):
            pairs = [(r, (r // near ^ step) * near + r % near) for r in range(rows)]
            x = x + lax.ppermute(x, "row", pairs)
        return x

    kept = None
    for tick in range(sections):
        if tick == 0:
            (gram,) = call(chain_gram, [gram_shape], [VMEM] * 5)(state, *own_parts)
            kept = gram
        elif tick < last:
            gram, kept = call(
                functools.partial(chain_gram_keep, tick),
                [gram_shape] * 2,
                [SMEM] + [VMEM] * 6,
            )(place, kept, state, *own_parts)
        else:
            (gram,) = call(
                functools.partial(chain_gram_last, tick), [gram_shape], [SMEM] + [VMEM] * 5
            )(place, state, *own_parts)
        body = functools.partial(chain_link_last, tick) if tick == last else chain_link
        (partial,) = call(body, [packed], [SMEM] + [VMEM] * 7)(
            place, gram, link, beside, *link_parts
        )
        pair = (tick, tick + 1) if tick < last else None
        count = near * (2 if pair else 1)
        arrived = exchange(partial.reshape(count, -1, half), pair)
        piece = over_far(arrived[:near].sum(axis=0))
        if tick == last:
            piece, u_before = lax.optimization_barrier((piece, u_before))
        copies = jnp.broadcast_to(piece[None], arrived.shape)
        state = exchange(copies, pair).reshape(partial.shape)
        link, beside = state, swapped(state[3 * half :])
        if tick == last - 1:
            u_own, x_own = call(
                factor_own,
                [square] * 2,
                [SMEM] + [HBM] * 2,
                scratch + [pltpu.VMEM(*gram_shape)] + [pltpu.VMEM(*square)] * 2,
                HBM,
            )(scalars(section, last), kept, state)
            state, u_own, x_own = lax.optimization_barrier((state, u_own, x_own))
            link = state
            u_before = lax.ppermute(u_own, "cores", [(k, k + 1) for k in range(last)])
            u_before = jnp.where(section == 0, up, u_before)

    both, x_own = call(
        factor_last, [((rank, 2 * rank), F32), square], [SMEM] + [VMEM] * 3, scratch
    )(scalars(section == last, which), state, beside, x_own)
    share = rank // sections
    tiles = both.reshape(sections, share, 2 * rank)
    sent = [lax.ppermute(tiles[k], "cores", [(last, k)]) for k in range(last)]
    (frames,) = call(
        functools.partial(frame, float(MODE * rank) ** 0.5), [(own.shape, F32)], [VMEM] * 3
    )(own, u_before, x_own)
    result = tiles[last]
    for k in range(last):
        result = jnp.where(section == k, sent[k], result)
    return frames[None, None], result[None, :, :rank], result[None, :, rank:]


def solution(mesh):
    in_specs = (P("tensor", "cores", "row", None, None), P("tensor", None, None))
    out_specs = (
        P("tensor", "cores", "row", None, None),
        P("tensor", "cores", None),
        P("tensor", "cores", None),
    )
    return jax.shard_map(shards, mesh=mesh, in_specs=in_specs, out_specs=out_specs, check_vma=False)
```

```python
import functools

import jax
import jax.numpy as jnp
from jax import lax
from jax.experimental import pallas as pl
from jax.experimental.pallas import tpu as pltpu
from jax.sharding import PartitionSpec as P

MODE = 128
LANES = 128
BLOCK = 64
GROUP = 8
VMEM_LIMIT = 16 * 1024 * 1024
F32 = jnp.float32
BF16 = jnp.bfloat16

VMEM = pl.BlockSpec(memory_space=pltpu.VMEM)
SMEM = pl.BlockSpec(memory_space=pltpu.SMEM)
HBM = pl.BlockSpec(memory_space=pltpu.HBM)


def call(body, outs, in_specs, scratch=(), out_spec=VMEM):
    return pl.pallas_call(
        body,
        out_shape=[jax.ShapeDtypeStruct(s, d) for s, d in outs],
        in_specs=in_specs,
        out_specs=[out_spec] * len(outs),
        scratch_shapes=list(scratch),
        compiler_params=pltpu.CompilerParams(vmem_limit_bytes=VMEM_LIMIT),
    )


def split(x):
    hi = x.astype(BF16)
    return hi, (x - hi.astype(F32)).astype(BF16)


def dot(a, b, dims=((1,), (0,))):
    return lax.dot_general(a, b, (dims, ((), ())), preferred_element_type=F32)


def dot3(a, b, dims=((1,), (0,))):
    (ah, al), (bh, bl) = a, b
    return dot(ah, bh, dims) + (dot(ah, bl, dims) + dot(al, bh, dims))


def full(a, b, dims=((1,), (0,))):
    return lax.dot_general(
        a, b, (dims, ((), ())), precision=lax.Precision.HIGHEST, preferred_element_type=F32
    )


def pack_gram(out, gram):
    half = gram.shape[0] // 2
    out[0:half, :] = gram[:half, :half]
    out[half : 2 * half, :] = gram[:half, half:]
    out[2 * half : 3 * half, :] = gram[half:, half:]


def gram_blocks(state):
    half = LANES
    return state[0:half, :], state[half : 2 * half, :], state[2 * half : 3 * half, :]


def whole_link(first, mine, theirs):
    return jnp.concatenate(
        [jnp.where(first, mine, theirs), jnp.where(first, theirs, mine)], axis=1
    )


def prepare_own(own, ch, cl, th, tl):
    modes, rank = own.shape[0], own.shape[1]
    for i in range(modes):
        at = pl.ds(i * rank, rank)
        mine = own[i]
        ch[:, at], cl[:, at] = split(mine)
        th[:, at], tl[:, at] = split(mine.T)


def prepare_link(which, own, other, th, tl, up, up_other, lh, ll, rh, rl, start, beside):
    modes, rank = own.shape[0], own.shape[1]
    half = rank // 2
    u, v = up[...], up_other[...]
    pack_gram(start, full(u, u, ((0,), (0,))))

    def sides(left, right, mine, theirs):
        link = full(left, right, ((0,), (0,)))
        start[3 * half :, :] = link[:, mine]
        beside[...] = link[:, theirs]

    low, high = slice(0, half), slice(half, rank)

    @pl.when(which[0] == 0)
    def _():
        lh[...] = th[...]
        ll[...] = tl[...]
        for i in range(modes):
            at = pl.ds(i * half, half)
            rh[:, at], rl[:, at] = split(other[i][:, low])
        sides(u, v, low, high)

    @pl.when(which[0] != 0)
    def _():
        for i in range(modes):
            at = pl.ds(i * half, half)
            rh[:, at], rl[:, at] = split(own[i][:, high])
            at = pl.ds(i * rank, rank)
            lh[:, at], ll[:, at] = split(other[i].T)
        sides(v, u, high, low)


def stacked(x, width):
    return jnp.concatenate(
        [x[:, i : i + width] for i in range(0, x.shape[1], width)], axis=0
    )


def chain_product(middle, right, left, width):
    mh, ml = split(dot3(middle, right))
    return dot3(left, (stacked(mh, width), stacked(ml, width)))


def chain_gram(tick, place, state, ch, cl, th, tl, out):
    rank = ch.shape[0]

    @pl.when(place[0] == tick)
    def _():
        a, b, c = gram_blocks(state)
        gram = jnp.concatenate(
            [jnp.concatenate([a, b], axis=1), jnp.concatenate([b.T, c], axis=1)], axis=0
        )
        pack_gram(
            out, chain_product(split(gram), (ch[...], cl[...]), (th[...], tl[...]), rank)
        )


def chain_gram_keep(tick, place, kept, state, ch, cl, th, tl, out, keep):
    mine = place[0] == tick - 1
    keep[...] = jnp.where(mine, state[: keep.shape[0], :], kept[...])
    chain_gram(tick, place, state, ch, cl, th, tl, out)


def chain_link(tick, place, which, gram, state, beside, lh, ll, rh, rl, out):
    rank = lh.shape[0]
    half = rank // 2

    @pl.when(place[0] == tick)
    def _():
        out[: 3 * half, :] = gram[...]
        link = whole_link(which[0] == 0, state[3 * half :, :], beside[...])
        out[3 * half :, :] = chain_product(
            split(link), (rh[...], rl[...]), (lh[...], ll[...]), half
        )


def eliminate(m, offset, n):
    rows = lax.broadcasted_iota(jnp.int32, (n, LANES), 0)
    lanes = lax.broadcasted_iota(jnp.int32, (n, LANES), 1)
    e = jnp.where(rows == lanes, 1.0, 0.0).astype(F32)
    done = []
    for g in range(0, n, GROUP):
        left = n - g
        at = lax.broadcasted_iota(jnp.int32, (left, LANES), 0)
        first = offset + g
        columns = [
            jnp.broadcast_to(m[:, first + k : first + k + 1], (left, LANES))
            for k in range(GROUP)
        ]
        for k in range(GROUP):
            pivot = columns[k][k : k + 1, :]
            f = jnp.where(at > k, columns[k] * (1.0 / pivot), 0.0)
            for l in range(k + 1, GROUP):
                columns[l] = columns[l] - f * columns[l][k : k + 1, :]
            root = lax.rsqrt(pivot)
            root = root * (1.5 - 0.5 * pivot * root * root)
            done.append(e[k : k + 1, :] * root)
            m = m - f * m[k : k + 1, :]
            e = e - f * e[k : k + 1, :]
        m, e = m[GROUP:], e[GROUP:]
    return jnp.concatenate(done, axis=0)


def factorize(u_out, x_out, work):
    rank = work.shape[0]
    for r in range(0, rank, BLOCK):
        tile, offset = r // LANES * LANES, r % LANES
        x = eliminate(work[r : r + BLOCK, tile : tile + LANES], offset, BLOCK)
        line = dot3(split(x[:, :BLOCK]), split(work[r : r + BLOCK, :]))
        row = lax.broadcasted_iota(jnp.int32, (BLOCK, rank), 0) + r
        column = lax.broadcasted_iota(jnp.int32, (BLOCK, rank), 1)
        upper = jnp.where(column >= row, line[:, :rank], 0.0)
        u_out[r : r + BLOCK, :rank] = upper
        x_out[r : r + BLOCK, :] = line[:, rank:]
        if r + BLOCK < rank:
            below = slice(r + BLOCK, rank)
            work[below, :] = work[below, :] - dot3(split(upper.T[below, :]), split(line))


def unpack_gram(state, work):
    rank = work.shape[0]
    half = rank // 2
    a, b, c = gram_blocks(state)
    work[:half, :half] = a
    work[:half, half:rank] = b
    work[half:, :half] = jnp.zeros_like(b)
    work[half:, half:rank] = c
    rows = lax.broadcasted_iota(jnp.int32, (rank, rank), 0)
    columns = lax.broadcasted_iota(jnp.int32, (rank, rank), 1)
    work[:, rank:] = jnp.where(rows == columns, 1.0, 0.0).astype(F32)


def factor_own(section, kept, state, u_out, x_out, work, gram, u, x):
    busy = section[0] < section[1]

    @pl.when(busy)
    def _():
        pltpu.sync_copy(kept, gram)

    @pl.when(section[0] == section[1] - 1)
    def _():
        pltpu.sync_copy(state.at[pl.ds(0, gram.shape[0])], gram)

    @pl.when(busy)
    def _():
        unpack_gram(gram, work)
        factorize(u, x, work)
        pltpu.sync_copy(u, u_out)
        pltpu.sync_copy(x, x_out)


def factor_last(flags, state, beside, x_own, both, x_out, work):
    rank = work.shape[0]

    @pl.when(flags[0] == 0)
    def _():
        x_out[...] = x_own[...]

    @pl.when(flags[0] != 0)
    def _():
        first = flags[1] == 0
        link = whole_link(first, state[3 * rank // 2 :, :], beside[...])
        both[:, rank:] = jnp.where(first, link, link.T)
        unpack_gram(state, work)
        factorize(both, x_out, work)


def frame(scale, own, upper, inverse, out):
    u = split(upper[...])
    x = split(inverse[...] * scale)
    for i in range(own.shape[0]):
        mixed = split(dot3(u, split(own[i])))
        out[i] = dot3(mixed, x, ((1,), (1,)))


def swapped(x):
    return lax.ppermute(x, "tensor", [(0, 1), (1, 0)])


def scalars(*values):
    return jnp.stack([jnp.asarray(v, jnp.int32) for v in values])


def shards(cores, incoming):
    own, up = cores[0, 0], incoming[0]
    modes, rank, _ = own.shape
    half = rank // 2
    section, which = lax.axis_index("cores"), lax.axis_index("tensor")
    sections, rows = lax.axis_size("cores"), lax.axis_size("row")
    last = sections - 1

    other, up_other = swapped(own), swapped(up)
    wide, narrow = ((rank, modes * rank), BF16), ((rank, modes * half), BF16)
    packed, side = ((3 * half + rank, half), F32), ((rank, half), F32)
    square = ((rank, rank), F32)
    scratch = [pltpu.VMEM((rank, 2 * rank), F32)]
    own_parts = call(prepare_own, [wide] * 4, [VMEM])(own)
    *link_parts, state, beside = call(
        prepare_link, [wide] * 2 + [narrow] * 2 + [packed, side], [SMEM] + [VMEM] * 6
    )(scalars(which), own, other, *own_parts[2:], up, up_other)
    gram_shape = ((3 * half, half), F32)
    near = max(1, rows // 4)
    far = rows // near
    place = scalars(section)

    def exchange(x, pair):
        blocks = [[g * near + j for j in range(near)] for g in range(far)]
        if pair is None:
            return lax.all_to_all(x, "row", 0, 0, tiled=True, axis_index_groups=blocks)
        rest = [k for k in range(sections) if k not in pair]
        groups = [[k * rows + r for k in p for r in b] for p in (pair, rest) for b in blocks]
        return lax.all_to_all(
            x, ("cores", "row"), 0, 0, tiled=True, axis_index_groups=groups
        )

    def over_far(x):
        terms = [x]
        for step in range(1, far):
            pairs = [(r, (r + step * near) % rows) for r in range(rows)]
            terms.append(lax.ppermute(x, "row", pairs))
        return sum(terms[2::2], terms[0]) + sum(terms[3::2], terms[1])

    kept = None
    for tick in range(sections):
        if 0 < tick < last:
            gram, kept = call(
                functools.partial(chain_gram_keep, tick),
                [gram_shape] * 2,
                [SMEM] + [VMEM] * 6,
            )(place, kept, state, *own_parts)
        else:
            (gram,) = call(
                functools.partial(chain_gram, tick), [gram_shape], [SMEM] + [VMEM] * 5
            )(place, state, *own_parts)
            kept = gram if tick == 0 else kept
        (partial,) = call(
            functools.partial(chain_link, tick), [packed], [SMEM] * 2 + [VMEM] * 7
        )(place, scalars(which), gram, state, beside, *link_parts)
        pair = (tick, tick + 1) if tick < last else None
        count = near * (2 if pair else 1)
        arrived = exchange(partial.reshape(count, -1, half), pair)
        piece = over_far(arrived[:near].sum(axis=0))
        copies = jnp.broadcast_to(piece[None], arrived.shape)
        state = exchange(copies, pair).reshape(partial.shape)
        beside = swapped(state[3 * half :])
        if tick == last - 1:
            u_own, x_own = call(
                factor_own,
                [square] * 2,
                [SMEM] + [HBM] * 2,
                scratch + [pltpu.VMEM(*gram_shape)] + [pltpu.VMEM(*square)] * 2,
                HBM,
            )(scalars(section, last), kept, state)
            state, u_own, x_own = lax.optimization_barrier((state, u_own, x_own))
            u_before = lax.ppermute(u_own, "cores", [(k, k + 1) for k in range(last)])
            u_before = jnp.where(section == 0, up, u_before)

    both, x_own = call(
        factor_last, [((rank, 2 * rank), F32), square], [SMEM] + [VMEM] * 3, scratch
    )(scalars(section == last, which), state, beside, x_own)
    share = rank // sections
    tiles = both.reshape(sections, share, 2 * rank)
    sent = [lax.ppermute(tiles[k], "cores", [(last, k)]) for k in range(last)]
    (frames,) = call(
        functools.partial(frame, float(MODE * rank) ** 0.5), [(own.shape, F32)], [VMEM] * 3
    )(own, u_before, x_own)
    result = tiles[last]
    for k in range(last):
        result = jnp.where(section == k, sent[k], result)
    return frames[None, None], result[None, :, :rank], result[None, :, rank:]


def solution(mesh):
    in_specs = (P("tensor", "cores", "row", None, None), P("tensor", None, None))
    out_specs = (
        P("tensor", "cores", "row", None, None),
        P("tensor", "cores", None),
        P("tensor", "cores", None),
    )
    return jax.shard_map(shards, mesh=mesh, in_specs=in_specs, out_specs=out_specs, check_vma=False)
```

```python
import functools

import jax
import jax.numpy as jnp
from jax import lax
from jax.experimental import pallas as pl
from jax.experimental.pallas import tpu as pltpu
from jax.sharding import PartitionSpec as P

MODE = 128
LANES = 128
BLOCK = 64
GROUP = 16
VMEM_LIMIT = 16 * 1024 * 1024
F32 = jnp.float32
BF16 = jnp.bfloat16

VMEM = pl.BlockSpec(memory_space=pltpu.VMEM)
SMEM = pl.BlockSpec(memory_space=pltpu.SMEM)
HBM = pl.BlockSpec(memory_space=pltpu.HBM)


def call(body, outs, in_specs, scratch=(), out_spec=VMEM):
    return pl.pallas_call(
        body,
        out_shape=[jax.ShapeDtypeStruct(s, d) for s, d in outs],
        in_specs=in_specs,
        out_specs=[out_spec] * len(outs),
        scratch_shapes=list(scratch),
        compiler_params=pltpu.CompilerParams(vmem_limit_bytes=VMEM_LIMIT),
    )


def split(x):
    hi = x.astype(BF16)
    return hi, (x - hi.astype(F32)).astype(BF16)


def dot(a, b, dims=((1,), (0,))):
    return lax.dot_general(a, b, (dims, ((), ())), preferred_element_type=F32)


def dot3(a, b, dims=((1,), (0,))):
    (ah, al), (bh, bl) = a, b
    return dot(ah, bh, dims) + (dot(ah, bl, dims) + dot(al, bh, dims))


def full(a, b, dims=((1,), (0,))):
    return lax.dot_general(
        a, b, (dims, ((), ())), precision=lax.Precision.HIGHEST, preferred_element_type=F32
    )


def pack_gram(out, gram):
    half = gram.shape[0] // 2
    out[0:half, :] = gram[:half, :half]
    out[half : 2 * half, :] = gram[:half, half:]
    out[2 * half : 3 * half, :] = gram[half:, half:]


def gram_blocks(state):
    half = LANES
    return state[0:half, :], state[half : 2 * half, :], state[2 * half : 3 * half, :]


def whole_link(first, mine, theirs):
    return jnp.concatenate(
        [jnp.where(first, mine, theirs), jnp.where(first, theirs, mine)], axis=1
    )


def prepare_own(own, ch, cl, th, tl):
    modes, rank = own.shape[0], own.shape[1]
    for i in range(modes):
        at = pl.ds(i * rank, rank)
        mine = own[i]
        ch[:, at], cl[:, at] = split(mine)
        th[:, at], tl[:, at] = split(mine.T)


def prepare_link(which, own, other, th, tl, up, up_other, lh, ll, rh, rl, start, beside):
    modes, rank = own.shape[0], own.shape[1]
    half = rank // 2
    u, v = up[...], up_other[...]
    pack_gram(start, full(u, u, ((0,), (0,))))

    def sides(left, right, mine, theirs):
        link = full(left, right, ((0,), (0,)))
        start[3 * half :, :] = link[:, mine]
        beside[...] = link[:, theirs]

    low, high = slice(0, half), slice(half, rank)

    @pl.when(which[0] == 0)
    def _():
        lh[...] = th[...]
        ll[...] = tl[...]
        for i in range(modes):
            at = pl.ds(i * half, half)
            rh[:, at], rl[:, at] = split(other[i][:, low])
        sides(u, v, low, high)

    @pl.when(which[0] != 0)
    def _():
        for i in range(modes):
            at = pl.ds(i * half, half)
            rh[:, at], rl[:, at] = split(own[i][:, high])
            at = pl.ds(i * rank, rank)
            lh[:, at], ll[:, at] = split(other[i].T)
        sides(v, u, high, low)


def stacked(x, width):
    return jnp.concatenate(
        [x[:, i : i + width] for i in range(0, x.shape[1], width)], axis=0
    )


def chain_product(middle, right, left, width):
    mh, ml = split(dot3(middle, right))
    return dot3(left, (stacked(mh, width), stacked(ml, width)))


def chain_gram(tick, place, state, ch, cl, th, tl, out):
    rank = ch.shape[0]

    @pl.when(place[0] == tick)
    def _():
        a, b, c = gram_blocks(state)
        gram = jnp.concatenate(
            [jnp.concatenate([a, b], axis=1), jnp.concatenate([b.T, c], axis=1)], axis=0
        )
        pack_gram(
            out, chain_product(split(gram), (ch[...], cl[...]), (th[...], tl[...]), rank)
        )


def chain_gram_keep(tick, place, kept, state, ch, cl, th, tl, out, keep):
    mine = place[0] == tick - 1
    keep[...] = jnp.where(mine, state[: keep.shape[0], :], kept[...])
    chain_gram(tick, place, state, ch, cl, th, tl, out)


def chain_link(tick, place, which, gram, state, beside, lh, ll, rh, rl, out):
    rank = lh.shape[0]
    half = rank // 2

    @pl.when(place[0] == tick)
    def _():
        out[: 3 * half, :] = gram[...]
        link = whole_link(which[0] == 0, state[3 * half :, :], beside[...])
        out[3 * half :, :] = chain_product(
            split(link), (rh[...], rl[...]), (lh[...], ll[...]), half
        )


def eliminate(m, offset, n):
    rows = lax.broadcasted_iota(jnp.int32, (n, LANES), 0)
    lanes = lax.broadcasted_iota(jnp.int32, (n, LANES), 1)
    e = jnp.where(rows == lanes, 1.0, 0.0).astype(F32)
    done = []
    for g in range(0, n, GROUP):
        left = n - g
        at = lax.broadcasted_iota(jnp.int32, (left, LANES), 0)
        first = offset + g
        columns = [
            jnp.broadcast_to(m[:, first + k : first + k + 1], (left, LANES))
            for k in range(GROUP)
        ]
        for k in range(GROUP):
            pivot = columns[k][k : k + 1, :]
            f = jnp.where(at > k, columns[k] * (1.0 / pivot), 0.0)
            for l in range(k + 1, GROUP):
                columns[l] = columns[l] - f * columns[l][k : k + 1, :]
            root = lax.rsqrt(pivot)
            root = root * (1.5 - 0.5 * pivot * root * root)
            done.append(e[k : k + 1, :] * root)
            m = m - f * m[k : k + 1, :]
            e = e - f * e[k : k + 1, :]
        m, e = m[GROUP:], e[GROUP:]
    return jnp.concatenate(done, axis=0)


def factorize(u_out, x_out, work):
    rank = work.shape[0]
    for r in range(0, rank, BLOCK):
        tile, offset = r // LANES * LANES, r % LANES
        x = eliminate(work[r : r + BLOCK, tile : tile + LANES], offset, BLOCK)
        line = dot3(split(x[:, :BLOCK]), split(work[r : r + BLOCK, :]))
        row = lax.broadcasted_iota(jnp.int32, (BLOCK, rank), 0) + r
        column = lax.broadcasted_iota(jnp.int32, (BLOCK, rank), 1)
        upper = jnp.where(column >= row, line[:, :rank], 0.0)
        u_out[r : r + BLOCK, :rank] = upper
        x_out[r : r + BLOCK, :] = line[:, rank:]
        if r + BLOCK < rank:
            below = slice(r + BLOCK, rank)
            work[below, :] = work[below, :] - dot3(split(upper.T[below, :]), split(line))


def unpack_gram(state, work):
    rank = work.shape[0]
    half = rank // 2
    a, b, c = gram_blocks(state)
    work[:half, :half] = a
    work[:half, half:rank] = b
    work[half:, :half] = jnp.zeros_like(b)
    work[half:, half:rank] = c
    rows = lax.broadcasted_iota(jnp.int32, (rank, rank), 0)
    columns = lax.broadcasted_iota(jnp.int32, (rank, rank), 1)
    work[:, rank:] = jnp.where(rows == columns, 1.0, 0.0).astype(F32)


def factor_own(section, kept, state, u_out, x_out, work, gram, u, x):
    busy = section[0] < section[1]

    @pl.when(busy)
    def _():
        pltpu.sync_copy(kept, gram)

    @pl.when(section[0] == section[1] - 1)
    def _():
        pltpu.sync_copy(state.at[pl.ds(0, gram.shape[0])], gram)

    @pl.when(busy)
    def _():
        unpack_gram(gram, work)
        factorize(u, x, work)
        pltpu.sync_copy(u, u_out)
        pltpu.sync_copy(x, x_out)


def factor_last(flags, state, beside, x_own, both, x_out, work):
    rank = work.shape[0]

    @pl.when(flags[0] == 0)
    def _():
        x_out[...] = x_own[...]

    @pl.when(flags[0] != 0)
    def _():
        first = flags[1] == 0
        link = whole_link(first, state[3 * rank // 2 :, :], beside[...])
        both[:, rank:] = jnp.where(first, link, link.T)
        unpack_gram(state, work)
        factorize(both, x_out, work)


def frame(scale, own, upper, inverse, out):
    u = split(upper[...])
    x = split(inverse[...] * scale)
    for i in range(own.shape[0]):
        mixed = split(dot3(u, split(own[i])))
        out[i] = dot3(mixed, x, ((1,), (1,)))


def swapped(x):
    return lax.ppermute(x, "tensor", [(0, 1), (1, 0)])


def scalars(*values):
    return jnp.stack([jnp.asarray(v, jnp.int32) for v in values])


def shards(cores, incoming):
    own, up = cores[0, 0], incoming[0]
    modes, rank, _ = own.shape
    half = rank // 2
    section, which = lax.axis_index("cores"), lax.axis_index("tensor")
    sections, rows = lax.axis_size("cores"), lax.axis_size("row")
    last = sections - 1

    other, up_other = swapped(own), swapped(up)
    wide, narrow = ((rank, modes * rank), BF16), ((rank, modes * half), BF16)
    packed, side = ((3 * half + rank, half), F32), ((rank, half), F32)
    square = ((rank, rank), F32)
    scratch = [pltpu.VMEM((rank, 2 * rank), F32)]
    own_parts = call(prepare_own, [wide] * 4, [VMEM])(own)
    *link_parts, state, beside = call(
        prepare_link, [wide] * 2 + [narrow] * 2 + [packed, side], [SMEM] + [VMEM] * 6
    )(scalars(which), own, other, *own_parts[2:], up, up_other)
    gram_shape = ((3 * half, half), F32)
    near = max(1, rows // 4)
    far = rows // near
    place = scalars(section)

    def exchange(x, pair):
        blocks = [[g * near + j for j in range(near)] for g in range(far)]
        if pair is None:
            return lax.all_to_all(x, "row", 0, 0, tiled=True, axis_index_groups=blocks)
        rest = [k for k in range(sections) if k not in pair]
        groups = [[k * rows + r for k in p for r in b] for p in (pair, rest) for b in blocks]
        return lax.all_to_all(
            x, ("cores", "row"), 0, 0, tiled=True, axis_index_groups=groups
        )

    def over_far(x):
        terms = [x]
        for step in range(1, far):
            pairs = [(r, (r + step * near) % rows) for r in range(rows)]
            terms.append(lax.ppermute(x, "row", pairs))
        return sum(terms[2::2], terms[0]) + sum(terms[3::2], terms[1])

    kept = None
    for tick in range(sections):
        if 0 < tick < last:
            gram, kept = call(
                functools.partial(chain_gram_keep, tick),
                [gram_shape] * 2,
                [SMEM] + [VMEM] * 6,
            )(place, kept, state, *own_parts)
        else:
            (gram,) = call(
                functools.partial(chain_gram, tick), [gram_shape], [SMEM] + [VMEM] * 5
            )(place, state, *own_parts)
            kept = gram if tick == 0 else kept
        (partial,) = call(
            functools.partial(chain_link, tick), [packed], [SMEM] * 2 + [VMEM] * 7
        )(place, scalars(which), gram, state, beside, *link_parts)
        pair = (tick, tick + 1) if tick < last else None
        count = near * (2 if pair else 1)
        arrived = exchange(partial.reshape(count, -1, half), pair)
        piece = over_far(arrived[:near].sum(axis=0))
        if tick == last:
            piece, u_before = lax.optimization_barrier((piece, u_before))
        copies = jnp.broadcast_to(piece[None], arrived.shape)
        state = exchange(copies, pair).reshape(partial.shape)
        beside = swapped(state[3 * half :])
        if tick == last - 1:
            u_own, x_own = call(
                factor_own,
                [square] * 2,
                [SMEM] + [HBM] * 2,
                scratch + [pltpu.VMEM(*gram_shape)] + [pltpu.VMEM(*square)] * 2,
                HBM,
            )(scalars(section, last), kept, state)
            state, u_own, x_own = lax.optimization_barrier((state, u_own, x_own))
            u_before = lax.ppermute(u_own, "cores", [(k, k + 1) for k in range(last)])
            u_before = jnp.where(section == 0, up, u_before)

    both, x_own = call(
        factor_last, [((rank, 2 * rank), F32), square], [SMEM] + [VMEM] * 3, scratch
    )(scalars(section == last, which), state, beside, x_own)
    share = rank // sections
    tiles = both.reshape(sections, share, 2 * rank)
    sent = [lax.ppermute(tiles[k], "cores", [(last, k)]) for k in range(last)]
    (frames,) = call(
        functools.partial(frame, float(MODE * rank) ** 0.5), [(own.shape, F32)], [VMEM] * 3
    )(own, u_before, x_own)
    result = tiles[last]
    for k in range(last):
        result = jnp.where(section == k, sent[k], result)
    return frames[None, None], result[None, :, :rank], result[None, :, rank:]


def solution(mesh):
    in_specs = (P("tensor", "cores", "row", None, None), P("tensor", None, None))
    out_specs = (
        P("tensor", "cores", "row", None, None),
        P("tensor", "cores", None),
        P("tensor", "cores", None),
    )
    return jax.shard_map(shards, mesh=mesh, in_specs=in_specs, out_specs=out_specs, check_vma=False)
```

```python
import functools

import jax
import jax.numpy as jnp
from jax import lax
from jax.experimental import pallas as pl
from jax.experimental.pallas import tpu as pltpu
from jax.sharding import PartitionSpec as P

MODE = 128
LANES = 128
BLOCK = 64
GROUP = 16
VMEM_LIMIT = 16 * 1024 * 1024
F32 = jnp.float32
BF16 = jnp.bfloat16

VMEM = pl.BlockSpec(memory_space=pltpu.VMEM)
SMEM = pl.BlockSpec(memory_space=pltpu.SMEM)
HBM = pl.BlockSpec(memory_space=pltpu.HBM)


def call(body, outs, in_specs, scratch=(), out_spec=VMEM):
    return pl.pallas_call(
        body,
        out_shape=[jax.ShapeDtypeStruct(s, d) for s, d in outs],
        in_specs=in_specs,
        out_specs=[out_spec] * len(outs),
        scratch_shapes=list(scratch),
        compiler_params=pltpu.CompilerParams(vmem_limit_bytes=VMEM_LIMIT),
    )


def split(x):
    hi = x.astype(BF16)
    return hi, (x - hi.astype(F32)).astype(BF16)


def dot(a, b, dims=((1,), (0,))):
    return lax.dot_general(a, b, (dims, ((), ())), preferred_element_type=F32)


def dot3(a, b, dims=((1,), (0,))):
    (ah, al), (bh, bl) = a, b
    return dot(ah, bh, dims) + (dot(ah, bl, dims) + dot(al, bh, dims))


def full(a, b, dims=((1,), (0,))):
    return lax.dot_general(
        a, b, (dims, ((), ())), precision=lax.Precision.HIGHEST, preferred_element_type=F32
    )


def pack_gram(out, gram):
    half = gram.shape[0] // 2
    out[0:half, :] = gram[:half, :half]
    out[half : 2 * half, :] = gram[:half, half:]
    out[2 * half : 3 * half, :] = gram[half:, half:]


def gram_blocks(state):
    half = LANES
    return state[0:half, :], state[half : 2 * half, :], state[2 * half : 3 * half, :]


def whole_link(first, mine, theirs):
    return jnp.concatenate(
        [jnp.where(first, mine, theirs), jnp.where(first, theirs, mine)], axis=1
    )


def prepare_own(own, ch, cl, th, tl):
    modes, rank = own.shape[0], own.shape[1]
    for i in range(modes):
        at = pl.ds(i * rank, rank)
        mine = own[i]
        ch[:, at], cl[:, at] = split(mine)
        th[:, at], tl[:, at] = split(mine.T)


def prepare_link(which, own, other, th, tl, up, up_other, lh, ll, rh, rl, start, beside):
    modes, rank = own.shape[0], own.shape[1]
    half = rank // 2
    u, v = up[...], up_other[...]
    pack_gram(start, full(u, u, ((0,), (0,))))

    def sides(left, right, mine, theirs):
        link = full(left, right, ((0,), (0,)))
        start[3 * half :, :] = link[:, mine]
        beside[...] = link[:, theirs]

    low, high = slice(0, half), slice(half, rank)

    @pl.when(which[0] == 0)
    def _():
        lh[...] = th[...]
        ll[...] = tl[...]
        for i in range(modes):
            at = pl.ds(i * half, half)
            rh[:, at], rl[:, at] = split(other[i][:, low])
        sides(u, v, low, high)

    @pl.when(which[0] != 0)
    def _():
        for i in range(modes):
            at = pl.ds(i * half, half)
            rh[:, at], rl[:, at] = split(own[i][:, high])
            at = pl.ds(i * rank, rank)
            lh[:, at], ll[:, at] = split(other[i].T)
        sides(v, u, high, low)


def stacked(x, width):
    return jnp.concatenate(
        [x[:, i : i + width] for i in range(0, x.shape[1], width)], axis=0
    )


def chain_product(middle, right, left, width):
    mh, ml = split(dot3(middle, right))
    return dot3(left, (stacked(mh, width), stacked(ml, width)))


def chain_gram(tick, place, state, ch, cl, th, tl, out):
    rank = ch.shape[0]

    @pl.when(place[0] == tick)
    def _():
        a, b, c = gram_blocks(state)
        gram = jnp.concatenate(
            [jnp.concatenate([a, b], axis=1), jnp.concatenate([b.T, c], axis=1)], axis=0
        )
        pack_gram(
            out, chain_product(split(gram), (ch[...], cl[...]), (th[...], tl[...]), rank)
        )


def chain_gram_keep(tick, place, kept, state, ch, cl, th, tl, out, keep):
    mine = place[0] == tick - 1
    keep[...] = jnp.where(mine, state[: keep.shape[0], :], kept[...])
    chain_gram(tick, place, state, ch, cl, th, tl, out)


def chain_link(tick, place, which, gram, state, beside, lh, ll, rh, rl, out):
    rank = lh.shape[0]
    half = rank // 2

    @pl.when(place[0] == tick)
    def _():
        out[: 3 * half, :] = gram[...]
        link = whole_link(which[0] == 0, state[3 * half :, :], beside[...])
        out[3 * half :, :] = chain_product(
            split(link), (rh[...], rl[...]), (lh[...], ll[...]), half
        )


def eliminate(m, offset, n):
    rows = lax.broadcasted_iota(jnp.int32, (n, LANES), 0)
    lanes = lax.broadcasted_iota(jnp.int32, (n, LANES), 1)
    e = jnp.where(rows == lanes, 1.0, 0.0).astype(F32)
    done = []
    for g in range(0, n, GROUP):
        left = n - g
        at = lax.broadcasted_iota(jnp.int32, (left, LANES), 0)
        first = offset + g
        columns = [
            jnp.broadcast_to(m[:, first + k : first + k + 1], (left, LANES))
            for k in range(GROUP)
        ]
        for k in range(GROUP):
            pivot = columns[k][k : k + 1, :]
            f = jnp.where(at > k, columns[k] * (1.0 / pivot), 0.0)
            for l in range(k + 1, GROUP):
                columns[l] = columns[l] - f * columns[l][k : k + 1, :]
            root = lax.rsqrt(pivot)
            root = root * (1.5 - 0.5 * pivot * root * root)
            done.append(e[k : k + 1, :] * root)
            m = m - f * m[k : k + 1, :]
            e = e - f * e[k : k + 1, :]
        m, e = m[GROUP:], e[GROUP:]
    return jnp.concatenate(done, axis=0)


def factorize(u_out, x_out, work):
    rank = work.shape[0]
    for r in range(0, rank, BLOCK):
        tile, offset = r // LANES * LANES, r % LANES
        x = eliminate(work[r : r + BLOCK, tile : tile + LANES], offset, BLOCK)
        line = dot3(split(x[:, :BLOCK]), split(work[r : r + BLOCK, :]))
        row = lax.broadcasted_iota(jnp.int32, (BLOCK, rank), 0) + r
        column = lax.broadcasted_iota(jnp.int32, (BLOCK, rank), 1)
        upper = jnp.where(column >= row, line[:, :rank], 0.0)
        u_out[r : r + BLOCK, :rank] = upper
        x_out[r : r + BLOCK, :] = line[:, rank:]
        if r + BLOCK < rank:
            below = slice(r + BLOCK, rank)
            work[below, :] = work[below, :] - dot3(split(upper.T[below, :]), split(line))


def unpack_gram(state, work):
    rank = work.shape[0]
    half = rank // 2
    a, b, c = gram_blocks(state)
    work[:half, :half] = a
    work[:half, half:rank] = b
    work[half:, :half] = jnp.zeros_like(b)
    work[half:, half:rank] = c
    rows = lax.broadcasted_iota(jnp.int32, (rank, rank), 0)
    columns = lax.broadcasted_iota(jnp.int32, (rank, rank), 1)
    work[:, rank:] = jnp.where(rows == columns, 1.0, 0.0).astype(F32)


def factor_own(section, kept, state, u_out, x_out, work, gram, u, x):
    busy = section[0] < section[1]

    @pl.when(busy)
    def _():
        pltpu.sync_copy(kept, gram)

    @pl.when(section[0] == section[1] - 1)
    def _():
        pltpu.sync_copy(state.at[pl.ds(0, gram.shape[0])], gram)

    @pl.when(busy)
    def _():
        unpack_gram(gram, work)
        factorize(u, x, work)
        pltpu.sync_copy(u, u_out)
        pltpu.sync_copy(x, x_out)


def factor_last(place, state, x_own, u_out, x_out, work):
    @pl.when(place[0] == 0)
    def _():
        x_out[...] = x_own[...]

    @pl.when(place[0] != 0)
    def _():
        unpack_gram(state, work)
        factorize(u_out, x_out, work)


def join(which, upper, state, beside, both):
    rank = upper.shape[0]
    first = which[0] == 0
    link = whole_link(first, state[3 * rank // 2 :, :], beside[...])
    both[:, :rank] = upper[...]
    both[:, rank:] = jnp.where(first, link, link.T)


def frame(scale, own, upper, inverse, out):
    u = split(upper[...])
    x = split(inverse[...] * scale)
    for i in range(own.shape[0]):
        mixed = split(dot3(u, split(own[i])))
        out[i] = dot3(mixed, x, ((1,), (1,)))


def swapped(x):
    return lax.ppermute(x, "tensor", [(0, 1), (1, 0)])


def scalars(*values):
    return jnp.stack([jnp.asarray(v, jnp.int32) for v in values])


def shards(cores, incoming):
    own, up = cores[0, 0], incoming[0]
    modes, rank, _ = own.shape
    half = rank // 2
    section, which = lax.axis_index("cores"), lax.axis_index("tensor")
    sections, rows = lax.axis_size("cores"), lax.axis_size("row")
    last = sections - 1

    other, up_other = swapped(own), swapped(up)
    wide, narrow = ((rank, modes * rank), BF16), ((rank, modes * half), BF16)
    packed, side = ((3 * half + rank, half), F32), ((rank, half), F32)
    square = ((rank, rank), F32)
    scratch = [pltpu.VMEM((rank, 2 * rank), F32)]
    own_parts = call(prepare_own, [wide] * 4, [VMEM])(own)
    *link_parts, state, beside = call(
        prepare_link, [wide] * 2 + [narrow] * 2 + [packed, side], [SMEM] + [VMEM] * 6
    )(scalars(which), own, other, *own_parts[2:], up, up_other)
    gram_shape = ((3 * half, half), F32)
    near = max(1, rows // 4)
    far = rows // near
    place = scalars(section)

    def exchange(x, pair):
        blocks = [[g * near + j for j in range(near)] for g in range(far)]
        if pair is None:
            return lax.all_to_all(x, "row", 0, 0, tiled=True, axis_index_groups=blocks)
        rest = [k for k in range(sections) if k not in pair]
        groups = [[k * rows + r for k in p for r in b] for p in (pair, rest) for b in blocks]
        return lax.all_to_all(
            x, ("cores", "row"), 0, 0, tiled=True, axis_index_groups=groups
        )

    def over_far(x):
        terms = [x]
        for step in range(1, far):
            pairs = [(r, (r + step * near) % rows) for r in range(rows)]
            terms.append(lax.ppermute(x, "row", pairs))
        return sum(terms[2::2], terms[0]) + sum(terms[3::2], terms[1])

    kept = None
    for tick in range(sections):
        if 0 < tick < last:
            gram, kept = call(
                functools.partial(chain_gram_keep, tick),
                [gram_shape] * 2,
                [SMEM] + [VMEM] * 6,
            )(place, kept, state, *own_parts)
        else:
            (gram,) = call(
                functools.partial(chain_gram, tick), [gram_shape], [SMEM] + [VMEM] * 5
            )(place, state, *own_parts)
            kept = gram if tick == 0 else kept
        (partial,) = call(
            functools.partial(chain_link, tick), [packed], [SMEM] * 2 + [VMEM] * 7
        )(place, scalars(which), gram, state, beside, *link_parts)
        pair = (tick, tick + 1) if tick < last else None
        count = near * (2 if pair else 1)
        arrived = exchange(partial.reshape(count, -1, half), pair)
        piece = over_far(arrived[:near].sum(axis=0))
        if tick == last:
            piece, u_before = lax.optimization_barrier((piece, u_before))
        copies = jnp.broadcast_to(piece[None], arrived.shape)
        state = exchange(copies, pair).reshape(partial.shape)
        beside = swapped(state[3 * half :])
        if tick == last - 1:
            u_own, x_own = call(
                factor_own,
                [square] * 2,
                [SMEM] + [HBM] * 2,
                scratch + [pltpu.VMEM(*gram_shape)] + [pltpu.VMEM(*square)] * 2,
                HBM,
            )(scalars(section, last), kept, state)
            state, u_own, x_own = lax.optimization_barrier((state, u_own, x_own))
            u_before = lax.ppermute(u_own, "cores", [(k, k + 1) for k in range(last)])
            u_before = jnp.where(section == 0, up, u_before)

    u_last, x_own = call(factor_last, [square] * 2, [SMEM] + [VMEM] * 2, scratch)(
        scalars(section == last), state, x_own
    )
    (both,) = call(join, [((rank, 2 * rank), F32)], [SMEM] + [VMEM] * 3)(
        scalars(which), u_last, state, beside
    )
    share = rank // sections
    tiles = both.reshape(sections, share, 2 * rank)
    sent = [lax.ppermute(tiles[k], "cores", [(last, k)]) for k in range(last)]
    (frames,) = call(
        functools.partial(frame, float(MODE * rank) ** 0.5), [(own.shape, F32)], [VMEM] * 3
    )(own, u_before, x_own)
    result = tiles[last]
    for k in range(last):
        result = jnp.where(section == k, sent[k], result)
    return frames[None, None], result[None, :, :rank], result[None, :, rank:]


def solution(mesh):
    in_specs = (P("tensor", "cores", "row", None, None), P("tensor", None, None))
    out_specs = (
        P("tensor", "cores", "row", None, None),
        P("tensor", "cores", None),
        P("tensor", "cores", None),
    )
    return jax.shard_map(shards, mesh=mesh, in_specs=in_specs, out_specs=out_specs, check_vma=False)
```
